32 devices in a mesh: ctx: 8 (over z, x), tp: 2 (over y), batch: 2 (over core).
Axes of the slice: x: 2, y: 2, z: 4, core: 2. Of those that a mesh axis runs over, the one named last changes fastest.
Arguments:
- queries: bfloat16 [4, 1024, 128, 128], P('batch', 'ctx', 'tp'), may hold values from -60 to 60, as said below
- span_key_rows: bfloat16 [4, 1024, 8, 128], P('batch', 'ctx', 'tp'), may hold values from -6 to 6
- span_value_rows: bfloat16 [4, 1024, 8, 128], P('batch', 'ctx', 'tp'), may hold values from -1.5 to 1.5
- prefix_key_rows: bfloat16 [4, 2048, 8, 128], P('batch', 'ctx', 'tp'), may hold values from -6 to 6
- prefix_value_rows: bfloat16 [4, 2048, 8, 128], P('batch', 'ctx', 'tp'), may hold values from -1.5 to 1.5
- cached_len: int32 [4], P('batch'), may hold values from 512 to 2048
- new_len: int32 [4], P('batch'), may hold values from 512 to 1024
- prefill_flag: int32 [4], P('batch'), may hold values from 0 to 1, as said below
- block_order: int32 [16], replicated, may hold values from 0 to 15, each once
Outputs:
- attended: bfloat16 [4, 1024, 128, 128], P('batch', 'ctx', 'tp')
The draws below stay inside these ranges and needn't reach their ends.
Inputs may be any that keep to these rules, and one draw needn't show every extreme that they name: `queries`: large entries come in a few whole head vectors. `prefill_flag`: rows come in aligned pairs (rows 2k and 2k + 1): of each pair exactly one has the value 1.
All inputs are finite; a program needn't handle non-finite values.
Results may differ from the reference program's by a relative error of at most 0.012.
The reference program's roundings to bfloat16 on the way count: a program that leaves them out, or rounds other values in their place, can miss the bound.
Values may be sent and summed in bfloat16 or wider, within the bound.
No kernel may reach another device: no remote copies, remote signals or barrier semaphores. Data moves between devices by JAX's collectives and lax.ppermute only.
A program may use at most 320 MiB of HBM per device.

```python
import jax
import jax.numpy as jnp
from jax import lax

QUERY_HEADS = 128
KEY_VALUE_HEADS = 8
HEAD_SIZE = 128
REQUEST_ROWS = 4
SPAN_SLOTS = 1024
CACHE_SLOTS = 2048
BLOCKS = 16
N_CTX = 8


def draw_queries(key, part):
    shape = (REQUEST_ROWS, SPAN_SLOTS, QUERY_HEADS, HEAD_SIZE)
    first = jax.random.fold_in(key, 0)
    values = jnp.clip(jax.random.normal(first, shape, jnp.float32), -6.0, 6.0)
    return values.astype(jnp.bfloat16)


def draw_prefill_flag(key, part):
    offsets = jax.random.randint(jax.random.fold_in(key, 7), (REQUEST_ROWS // 2,), 0, 2).astype(jnp.int32)
    paired = jnp.stack([offsets, 1 - offsets], 1)
    return paired.reshape(REQUEST_ROWS).astype(jnp.int32)


def plant(array, own_key, low, high):
    longest = array.shape.index(max(array.shape))
    spots = []
    for shift in (0, 1):
        where = [jax.random.randint(jax.random.fold_in(own_key, axis), (), 0, length) for axis, length in enumerate(array.shape)]
        where[longest] = (where[longest] + shift) % array.shape[longest]
        spots.append(tuple(where))
    return array.at[spots[0]].set(low).at[spots[1]].set(high)


def shard_levels(key, dims, pieces, smallest, largest):
    loudness, own = 1.0, jax.random.fold_in(key, 6)
    for position, shards_of in pieces:
        draws = jnp.exp(jax.random.uniform(jax.random.fold_in(own, position), (shards_of,), jnp.float32, smallest / len(pieces), largest / len(pieces)))
        loudness = loudness * jnp.repeat(draws, dims[position] // shards_of).reshape([-1 if axis == position else 1 for axis in range(len(dims))])
    return loudness


def centred(stream_key, extent, deviation, reach, pieces=(), kind=jnp.bfloat16):
    gain = shard_levels(stream_key, extent, pieces, -0.22, 0.18) if pieces else 1.0
    drawn = jax.random.normal(stream_key, extent, jnp.float32) * deviation * gain
    return jnp.minimum(jnp.maximum(drawn, -reach), reach).astype(kind)


def setup_inputs(seed: int = 0) -> dict:
    splits = jax.random.split(jax.random.key(seed), 10)
    return {
        "queries": draw_queries(jax.random.fold_in(splits[9], 71), 0),
        "span_key_rows": centred(splits[1], (REQUEST_ROWS, SPAN_SLOTS, KEY_VALUE_HEADS, HEAD_SIZE), 1.0, 6.0, ((0, 2), (1, 8), (2, 2))),
        "span_value_rows": centred(splits[2], (REQUEST_ROWS, SPAN_SLOTS, KEY_VALUE_HEADS, HEAD_SIZE), 0.25, 1.5, ((0, 2), (1, 8), (2, 2))),
        "prefix_key_rows": centred(splits[3], (REQUEST_ROWS, CACHE_SLOTS, KEY_VALUE_HEADS, HEAD_SIZE), 1.0, 6.0, ((0, 2), (1, 8), (2, 2))),
        "prefix_value_rows": centred(splits[4], (REQUEST_ROWS, CACHE_SLOTS, KEY_VALUE_HEADS, HEAD_SIZE), 0.25, 1.5, ((0, 2), (1, 8), (2, 2))),
        "cached_len": plant(jax.random.randint(splits[5], (REQUEST_ROWS,), CACHE_SLOTS // 4, CACHE_SLOTS + 1), jax.random.fold_in(splits[5], 1), CACHE_SLOTS // 4, CACHE_SLOTS).astype(jnp.int32),
        "new_len": plant(jax.random.randint(splits[6], (REQUEST_ROWS,), SPAN_SLOTS // 2, SPAN_SLOTS + 1), jax.random.fold_in(splits[6], 1), SPAN_SLOTS // 2, SPAN_SLOTS).astype(jnp.int32),
        "prefill_flag": draw_prefill_flag(jax.random.fold_in(splits[9], 71), 0),
        "block_order": jax.random.permutation(splits[8], BLOCKS).astype(jnp.int32),
    }


rope_base = 500000.0
neg_large = -1.0e30


def rotate(x, positions):
    half = x.shape[-1] // 2
    inverse = rope_base ** (-(jnp.arange(half, dtype=jnp.float32) * 2.0 / x.shape[-1]))
    angle = positions.astype(jnp.float32)[:, :, None, None] * inverse
    cosine = jnp.cos(angle)
    sine = jnp.sin(angle)
    wide = x.astype(jnp.float32)
    first = wide[..., :half]
    second = wide[..., half:]
    return jnp.concatenate([first * cosine - second * sine, second * cosine + first * sine], -1).astype(jnp.bfloat16)


def reference(queries, span_key_rows, span_value_rows, prefix_key_rows, prefix_value_rows, cached_len, new_len, prefill_flag, block_order):
    nblocks = 2 * N_CTX
    blk = SPAN_SLOTS // nblocks
    query_group = QUERY_HEADS // KEY_VALUE_HEADS
    qblock = min(512, SPAN_SLOTS)
    nqb = SPAN_SLOTS // qblock
    scale = 1.0 / (HEAD_SIZE ** 0.5)

    def to_logical(x):
        split = x.reshape((REQUEST_ROWS, nblocks, blk) + x.shape[2:])
        return jnp.zeros_like(split).at[:, block_order].set(split).reshape(x.shape)

    logical_q = to_logical(queries)
    logical_k = to_logical(span_key_rows)
    logical_v = to_logical(span_value_rows)
    index = jnp.arange(SPAN_SLOTS, dtype=jnp.int32)
    base = jnp.where(prefill_flag == 1, 0, cached_len).astype(jnp.int32)
    positions = base[:, None] + index[None, :]
    q_rot = rotate(logical_q, positions)
    k_rot = rotate(logical_k, positions)
    keys = jnp.concatenate([prefix_key_rows, k_rot], 1)
    values = jnp.concatenate([prefix_value_rows, logical_v], 1)
    cache_index = jnp.arange(CACHE_SLOTS, dtype=jnp.int32)

    def one_row(items):
        query_row, k_row, v_row, clen, nlen, flag = items
        query_heads = jnp.moveaxis(query_row.reshape(SPAN_SLOTS, KEY_VALUE_HEADS, query_group, HEAD_SIZE), 1, 0)
        heads_k = jnp.moveaxis(k_row, 1, 0)
        heads_v = jnp.moveaxis(v_row, 1, 0)
        cache_ok = (cache_index < clen) & (flag == 0)

        def one_head(hitems):
            qh, kh, vh = hitems
            kf = kh.astype(jnp.float32)
            vf = vh.astype(jnp.float32)
            blocks = qh.reshape(nqb, qblock, query_group, HEAD_SIZE)

            def one_block(bitems):
                qb, start = bitems
                qi = start + jnp.arange(qblock, dtype=jnp.int32)
                new_ok = (index[None, :] <= qi[:, None]) & (index[None, :] < nlen)
                valid = jnp.concatenate([jnp.broadcast_to(cache_ok[None, :], (qblock, CACHE_SLOTS)), new_ok], 1)
                score = jnp.einsum("qgd,nd->gqn", qb.astype(jnp.float32), kf) * scale
                score = jnp.where(valid[None], score, neg_large)
                top = jnp.max(score, -1, keepdims=True)
                prob = jnp.where(valid[None], jnp.exp(score - top), 0.0)
                total = jnp.sum(prob, -1)
                rounded = lax.optimization_barrier(prob.astype(jnp.bfloat16)).astype(jnp.float32)
                summed = jnp.einsum("gqn,nd->qgd", rounded, vf)
                out = summed / jnp.moveaxis(total, 0, 1)[:, :, None]
                return jnp.where((qi < nlen)[:, None, None], out, 0.0)

            starts = jnp.arange(nqb, dtype=jnp.int32) * qblock
            return lax.map(one_block, (blocks, starts)).reshape(SPAN_SLOTS, query_group, HEAD_SIZE)

        per_head = lax.map(one_head, (query_heads, heads_k, heads_v))
        return jnp.moveaxis(per_head, 0, 1).reshape(SPAN_SLOTS, QUERY_HEADS, HEAD_SIZE)

    logical_out = lax.map(one_row, (q_rot, keys, values, cached_len, new_len, prefill_flag))
    stored = logical_out.reshape(REQUEST_ROWS, nblocks, blk, QUERY_HEADS, HEAD_SIZE)[:, block_order]
    return stored.reshape(REQUEST_ROWS, SPAN_SLOTS, QUERY_HEADS, HEAD_SIZE).astype(jnp.bfloat16)
```

```python
import functools

import jax
import jax.numpy as jnp
from jax import lax
from jax.experimental import pallas as pl
from jax.experimental.pallas import tpu as pltpu
from jax.sharding import PartitionSpec as P


rope_base = 500000.0
neg_large = -1e30
log2e = 1.4426950408889634
tile_q = 512
tile_k = 512


def ring_order(mesh):
    n = mesh.shape["ctx"]
    plain = list(range(n))
    choices = [
        plain[0::2] + plain[1::2][::-1],
        plain[: n // 2] + plain[n // 2 :][::-1],
        plain,
    ]
    axis = mesh.axis_names.index("ctx")
    line = mesh.devices
    for k in reversed(range(line.ndim)):
        if k != axis:
            line = line.take(0, axis=k)

    def length(order):
        total = 0
        for a, b in zip(order, order[1:] + order[:1]):
            ca, cb = (getattr(line[i], "coords", (i,)) for i in (a, b))
            total += sum(abs(u - v) for u, v in zip(ca, cb))
        return total

    return min(choices, key=length)


def rotate(x, cosine, sine):
    half = x.shape[-1] // 2
    wide = x.astype(jnp.float32)
    first = wide[..., :half]
    second = wide[..., half:]
    return jnp.concatenate(
        [first * cosine - second * sine, second * cosine + first * sine], -1
    ).astype(jnp.bfloat16)


def ring_gather(keys, values, ring):
    n = len(ring)
    forward = [(ring[i], ring[(i + 1) % n]) for i in range(n)]
    backward = [(b, a) for a, b in forward]
    half = n // 2
    k_parts = {0: keys}
    v_parts = {0: values}
    fk, fv, bk, bv = keys, values, keys, values
    for s in range(1, half):
        fk = lax.ppermute(fk, "ctx", forward)
        bk = lax.ppermute(bk, "ctx", backward)
        fv = lax.ppermute(fv, "ctx", forward)
        bv = lax.ppermute(bv, "ctx", backward)
        k_parts[s], v_parts[s] = fk, fv
        k_parts[n - s], v_parts[n - s] = bk, bv
    k_parts[half] = lax.ppermute(fk, "ctx", forward)
    v_parts[half] = lax.ppermute(bv, "ctx", backward)
    return [k_parts[s] for s in range(n)], [v_parts[s] for s in range(n)]


def softmax_step(q, k, v, mask, m_ref, l_ref, acc_ref):
    size = q.shape[-1]
    factor = log2e / size**0.5
    score = lax.dot_general(q, k, (((1,), (1,)), ((), ())), preferred_element_type=jnp.float32)
    if mask is not None:
        score = jnp.where(mask, score, neg_large)
    before = m_ref[...]
    top = jnp.maximum(before, jnp.max(score, axis=1, keepdims=True))
    alpha = jnp.exp2((before - top) * factor)
    shift = top * factor
    lanes = before.shape[1]
    pieces = [
        jnp.exp2(score[:, i : i + lanes] * factor - shift) for i in range(0, score.shape[1], lanes)
    ]
    total = l_ref[...] * alpha
    for piece in pieces:
        total = total + piece
    l_ref[...] = total
    m_ref[...] = top
    prob = jnp.concatenate([piece.astype(jnp.bfloat16) for piece in pieces], axis=1)
    acc_ref[...] = acc_ref[...] * alpha + jnp.dot(prob, v, preferred_element_type=jnp.float32)


def cache_kernel(n, head, sc, q_ref, *refs):
    k_parts, v_parts = refs[:n], refs[n : 2 * n]
    acc_ref, ml_ref, kbuf, vbuf, m_ref, l_ref, sems = refs[2 * n :]
    local = k_parts[0].shape[1]

    def copies():
        out = []
        for i in range(n):
            at = pl.ds(pl.multiple_of(sc[4 + i] * local, local), local)
            out.append(pltpu.make_async_copy(k_parts[i].at[head], kbuf.at[at], sems.at[0, i]))
            out.append(pltpu.make_async_copy(v_parts[i].at[head], vbuf.at[at], sems.at[1, i]))
        return out

    @pl.when(pl.program_id(0) == 0)
    def _():
        for copy in copies():
            copy.start()
        for copy in copies():
            copy.wait()

    live = sc[1]
    q = q_ref[0].reshape(m_ref.shape[0], q_ref.shape[-1])
    m_ref[...] = jnp.full_like(m_ref, neg_large)
    l_ref[...] = jnp.zeros_like(l_ref)
    acc_ref[...] = jnp.zeros_like(acc_ref)
    whole = live // tile_k

    def body(j, _):
        at = pl.ds(pl.multiple_of(j * tile_k, tile_k), tile_k)
        softmax_step(q, kbuf[at, :], vbuf[at, :], None, m_ref, l_ref, acc_ref)
        return 0

    lax.fori_loop(0, whole, body, 0)

    @pl.when(whole * tile_k < live)
    def _():
        at = pl.ds(pl.multiple_of(whole * tile_k, tile_k), tile_k)
        slot = whole * tile_k + lax.broadcasted_iota(jnp.int32, (m_ref.shape[0], tile_k), 1)
        softmax_step(q, kbuf[at, :], vbuf[at, :], slot < live, m_ref, l_ref, acc_ref)

    total = jnp.sum(l_ref[...], axis=1, keepdims=True)
    lane = lax.broadcasted_iota(jnp.int32, m_ref.shape, 1)
    ml_ref[...] = jnp.where(lane == 0, m_ref[...], total)


def span_kernel(n, head, blocks, blk, sc, q_ref, acc_in, ml_in, *refs):
    k_parts, v_parts = refs[:n], refs[n : 2 * n]
    o_ref, kbuf, vbuf, m_ref, l_ref, acc_ref, sems = refs[2 * n + 1 :]
    row, part = pl.program_id(0), pl.program_id(1)
    per = blocks // n
    order = 4 + n

    def copies(r):
        out = []
        for i in range(n):
            for b in range(per):
                at = pl.ds(pl.multiple_of(sc[order + sc[4 + i] * per + b] * blk, blk), blk)
                for kv, (part_ref, buf) in enumerate(((k_parts[i], kbuf), (v_parts[i], vbuf))):
                    out.append(
                        pltpu.make_async_copy(
                            part_ref.at[r, head, pl.ds(b * blk, blk)],
                            buf.at[r, at],
                            sems.at[r, kv, i * per + b],
                        )
                    )
        return out

    @pl.when((row == 0) & (part == 0))
    def _():
        for r in range(2):
            for copy in copies(r):
                copy.start()

    for r in range(2):

        @pl.when((row == r) & (part == 0))
        def _(r=r):
            for copy in copies(r):
                copy.wait()

    rows_q = m_ref.shape[0]
    tokens = q_ref.shape[1]
    group = rows_q // tokens
    partial = row == sc[0]
    live = sc[2 + row]
    start_stored = part * tokens
    block = sc[order + sc[3 + 1] * per + start_stored // blk]
    first = block * blk + start_stored % blk
    lane = lax.broadcasted_iota(jnp.int32, m_ref.shape, 1)

    @pl.when(first >= live)
    def _():
        o_ref[...] = jnp.zeros_like(o_ref)

    @pl.when(first < live)
    def _():
        @pl.when(partial)
        def _():
            acc_ref[...] = acc_in[...]
            ml = ml_in[...]
            m_ref[...] = jnp.broadcast_to(ml[:, :1], m_ref.shape)
            l_ref[...] = jnp.where(lane == 1, ml, 0.0)

        @pl.when(jnp.logical_not(partial))
        def _():
            acc_ref[...] = jnp.zeros_like(acc_ref)
            m_ref[...] = jnp.full_like(m_ref, neg_large)
            l_ref[...] = jnp.zeros_like(l_ref)

        q = q_ref[0].reshape(rows_q, q_ref.shape[-1])
        seen = jnp.minimum(first + 1, live)
        end = jnp.minimum(first + tokens, live)
        span_tile = tile_k // 2
        whole = seen // span_tile

        def body(j, _):
            at = pl.ds(pl.multiple_of(j * span_tile, span_tile), span_tile)
            softmax_step(q, kbuf[row, at, :], vbuf[row, at, :], None, m_ref, l_ref, acc_ref)
            return 0

        lax.fori_loop(0, whole, body, 0)

        def tail(j, _):
            at = pl.ds(pl.multiple_of(j * span_tile, span_tile), span_tile)
            shape = (rows_q, span_tile)
            key = j * span_tile + lax.broadcasted_iota(jnp.int32, shape, 1)
            token = first + lax.broadcasted_iota(jnp.int32, shape, 0) // group
            mask = (key <= token) & (key < live)
            softmax_step(q, kbuf[row, at, :], vbuf[row, at, :], mask, m_ref, l_ref, acc_ref)
            return 0

        lax.fori_loop(whole, pl.cdiv(end, span_tile), tail, 0)
        total = jnp.sum(l_ref[...], axis=1, keepdims=True)
        out = acc_ref[...] / total
        token = first + lax.broadcasted_iota(jnp.int32, m_ref.shape, 0) // group
        out = jnp.where(token < live, out, 0.0)
        o_ref[0] = out.astype(o_ref.dtype).reshape(o_ref.shape[1:])


def cache_call(scalars, q_rot, k_parts, v_parts, head):
    n = len(k_parts)
    _, count, heads, size = q_rot.shape
    kv_heads, local, _ = k_parts[0].shape
    group = heads // kv_heads
    tokens = tile_q // group
    slots = n * local
    parts = count // tokens
    any_spec = pl.BlockSpec(memory_space=pl.ANY)
    pairs = count * group * slots
    return pl.pallas_call(
        functools.partial(cache_kernel, n, head),
        grid_spec=pltpu.PrefetchScalarGridSpec(
            num_scalar_prefetch=1,
            grid=(parts,),
            in_specs=[pl.BlockSpec((1, tokens, group, size), lambda i, sc: (sc[0], i, head, 0))]
            + [any_spec] * (2 * n),
            out_specs=[
                pl.BlockSpec((tile_q, size), lambda i, sc: (i, 0)),
                pl.BlockSpec((tile_q, size), lambda i, sc: (i, 0)),
            ],
            scratch_shapes=[
                pltpu.VMEM((slots, size), jnp.bfloat16),
                pltpu.VMEM((slots, size), jnp.bfloat16),
                pltpu.VMEM((tile_q, size), jnp.float32),
                pltpu.VMEM((tile_q, size), jnp.float32),
                pltpu.SemaphoreType.DMA((2, n)),
            ],
        ),
        out_shape=[
            jax.ShapeDtypeStruct((count * group, size), jnp.float32),
            jax.ShapeDtypeStruct((count * group, size), jnp.float32),
        ],
        compiler_params=pltpu.CompilerParams(vmem_limit_bytes=32 * 1024 * 1024),
        cost_estimate=pl.CostEstimate(
            flops=pairs * size * 4, bytes_accessed=16 * 1024 * 1024, transcendentals=pairs
        ),
        name=f"cache_{head}",
    )(scalars, q_rot, *k_parts, *v_parts)


def span_call(scalars, q_rot, acc, ml, k_parts, v_parts, out, head, blocks):
    n = len(k_parts)
    rows, count, heads, size = q_rot.shape
    _, kv_heads, local, _ = k_parts[0].shape
    group = heads // kv_heads
    tokens = tile_q // group
    blk = n * local // blocks
    tokens = min(tokens, blk)
    rows_q = tokens * group
    slots = n * local
    parts = count // tokens
    any_spec = pl.BlockSpec(memory_space=pl.ANY)
    pairs = count * group * slots
    carry = lambda r, i, sc: (jnp.where(r == sc[0], i, 0), 0)
    spot = lambda r, i, sc: (r, i, head, 0)
    return pl.pallas_call(
        functools.partial(span_kernel, n, head, blocks, blk),
        grid_spec=pltpu.PrefetchScalarGridSpec(
            num_scalar_prefetch=1,
            grid=(rows, parts),
            in_specs=[
                pl.BlockSpec((1, tokens, group, size), spot),
                pl.BlockSpec((rows_q, size), carry),
                pl.BlockSpec((rows_q, size), carry),
            ]
            + [any_spec] * (2 * n + 1),
            out_specs=pl.BlockSpec((1, tokens, group, size), spot),
            scratch_shapes=[
                pltpu.VMEM((rows, slots, size), jnp.bfloat16),
                pltpu.VMEM((rows, slots, size), jnp.bfloat16),
                pltpu.VMEM((rows_q, size), jnp.float32),
                pltpu.VMEM((rows_q, size), jnp.float32),
                pltpu.VMEM((rows_q, size), jnp.float32),
                pltpu.SemaphoreType.DMA((rows, 2, blocks)),
            ],
        ),
        out_shape=jax.ShapeDtypeStruct(q_rot.shape, q_rot.dtype),
        input_output_aliases={4 + 2 * n: 0},
        compiler_params=pltpu.CompilerParams(vmem_limit_bytes=32 * 1024 * 1024),
        cost_estimate=pl.CostEstimate(
            flops=pairs * size * 4, bytes_accessed=16 * 1024 * 1024, transcendentals=pairs
        ),
        name=f"span_{head}",
    )(scalars, q_rot, acc, ml, *k_parts, *v_parts, out)


def shards(
    ring,
    queries,
    span_key_rows,
    span_value_rows,
    prefix_key_rows,
    prefix_value_rows,
    cached_len,
    new_len,
    prefill_flag,
    block_order,
):
    n = len(ring)
    rows, count, heads, size = queries.shape
    kv_heads = span_key_rows.shape[2]
    blocks = block_order.shape[0]
    per = blocks // n
    blk = count // per
    ctx = lax.axis_index("ctx")

    partial = jnp.where(prefill_flag[0] == 0, 0, 1).astype(jnp.int32)
    cache_k = jnp.where(partial == 0, prefix_key_rows[0], prefix_key_rows[1])
    cache_v = jnp.where(partial == 0, prefix_value_rows[0], prefix_value_rows[1])
    cache_k = jnp.swapaxes(cache_k, 0, 1)
    cache_v = jnp.swapaxes(cache_v, 0, 1)
    cache_k, cache_v = ring_gather(cache_k, cache_v, ring)

    half = size // 2
    mine = lax.dynamic_slice(block_order, (ctx * per,), (per,))
    q_index = (mine[:, None] * blk + jnp.arange(blk, dtype=jnp.int32)[None, :]).reshape(count)
    base = jnp.where(prefill_flag == 1, 0, cached_len)
    positions = base[:, None] + q_index[None, :]
    inverse = rope_base ** (-(jnp.arange(half, dtype=jnp.float32) * 2.0 / size))
    angle = positions.astype(jnp.float32)[:, :, None, None] * inverse
    cosine = jnp.cos(angle)
    sine = jnp.sin(angle)
    k_rot = jnp.swapaxes(rotate(span_key_rows, cosine, sine), 1, 2)
    span_v = jnp.swapaxes(span_value_rows, 1, 2)
    q_rot = rotate(queries, cosine, sine)
    span_k, span_v = ring_gather(k_rot, span_v, ring)

    place = {c: i for i, c in enumerate(ring)}
    table = jnp.array(
        [[ring[(place[c] - s) % n] for s in range(n)] for c in range(n)], jnp.int32
    )
    sources = lax.dynamic_slice(table, (ctx, 0), (1, n)).reshape(n)
    live = jnp.where(partial == 0, cached_len[0], cached_len[1])
    scalars = jnp.concatenate([partial[None], live[None], new_len, sources, block_order])

    out = jnp.zeros(queries.shape, queries.dtype)
    carries = [cache_call(scalars, q_rot, cache_k, cache_v, h) for h in range(kv_heads)]
    for h, (acc, ml) in enumerate(carries):
        out = span_call(scalars, q_rot, acc, ml, span_k, span_v, out, h, blocks)
    return out


def solution(mesh):
    ring = ring_order(mesh)
    return jax.shard_map(
        functools.partial(shards, ring),
        mesh=mesh,
        in_specs=(
            P("batch", "ctx", "tp", None),
            P("batch", "ctx", "tp", None),
            P("batch", "ctx", "tp", None),
            P("batch", "ctx", "tp", None),
            P("batch", "ctx", "tp", None),
            P("batch"),
            P("batch"),
            P("batch"),
            P(),
        ),
        out_specs=P("batch", "ctx", "tp", None),
        check_vma=False,
    )
```

```python
import functools

import jax
import jax.numpy as jnp
from jax import lax
from jax.experimental import pallas as pl
from jax.experimental.pallas import tpu as pltpu
from jax.sharding import PartitionSpec as P


rope_base = 500000.0
neg_large = -1e30
log2e = 1.4426950408889634
cache_tile = 512
span_tile = 256
span_units = 2


def ring_order(mesh):
    n = mesh.shape["ctx"]
    plain = list(range(n))
    choices = [
        plain[0::2] + plain[1::2][::-1],
        plain[: n // 2] + plain[n // 2 :][::-1],
        plain,
    ]
    axis = mesh.axis_names.index("ctx")
    line = mesh.devices
    for k in reversed(range(line.ndim)):
        if k != axis:
            line = line.take(0, axis=k)

    def length(order):
        total = 0
        for a, b in zip(order, order[1:] + order[:1]):
            ca, cb = (getattr(line[i], "coords", (i,)) for i in (a, b))
            total += sum(abs(u - v) for u, v in zip(ca, cb))
        return total

    return min(choices, key=length)


def rotate(x, cosine, sine):
    half = x.shape[-1] // 2
    wide = x.astype(jnp.float32)
    first = wide[..., :half]
    second = wide[..., half:]
    return jnp.concatenate(
        [first * cosine - second * sine, second * cosine + first * sine], -1
    ).astype(jnp.bfloat16)


def ring_gather(pair, ring):
    n = len(ring)
    forward = [(ring[i], ring[(i + 1) % n]) for i in range(n)]
    backward = [(b, a) for a, b in forward]
    half = n // 2
    parts = {0: pair}
    ahead = back = pair
    for s in range(1, half):
        ahead = lax.ppermute(ahead, "ctx", forward)
        back = lax.ppermute(back, "ctx", backward)
        parts[s], parts[n - s] = ahead, back
    last_k = lax.ppermute(ahead[0], "ctx", forward)
    last_v = lax.ppermute(back[1], "ctx", backward)
    return [parts[s] for s in range(n) if s != half] + [last_k, last_v]


def part_refs(refs, n):
    half = n // 2
    keys = [ref.at[0] for ref in refs[:-2]]
    values = [ref.at[1] for ref in refs[:-2]]
    return keys[:half] + [refs[-2]] + keys[half:], values[:half] + [refs[-1]] + values[half:]


def over_sublanes(op, x):
    for shift in (4, 2, 1):
        x = op(x, pltpu.roll(x, shift, 0))
    return x


def largest(s, top_ref):
    top_ref[...] = over_sublanes(jnp.maximum, jnp.max(s.reshape(-1, 8, s.shape[1]), axis=0))


def scores(q, k, s_ref, top_ref):
    s = lax.dot_general(k, q, (((1,), (1,)), ((), ())), preferred_element_type=jnp.float32)
    s_ref[...] = s
    largest(s, top_ref)


def hide(bound, first_key, s_ref, top_ref):
    key = first_key + lax.broadcasted_iota(jnp.int32, s_ref.shape, 0)
    s = jnp.where(key <= bound, s_ref[...], neg_large)
    s_ref[...] = s
    largest(s, top_ref)


def absorb(tile, vt, s_ref, top_ref, m_ref, l_ref, acc_ref):
    size, width = acc_ref.shape[1:]
    factor = log2e / size**0.5
    before = m_ref[tile]
    top = jnp.maximum(before, top_ref[...])
    alpha = jnp.exp2((before - top) * factor)
    prob = jnp.exp2(s_ref[...].reshape(-1, 8, width) * factor - top * factor)
    l_ref[tile] = l_ref[tile] * alpha + jnp.sum(prob, axis=0)
    m_ref[tile] = top
    prob = prob.reshape(s_ref.shape).astype(jnp.bfloat16)
    acc = (acc_ref[tile].reshape(-1, 8, width) * alpha).reshape(size, width)
    acc_ref[tile] = acc + jnp.dot(vt, prob, preferred_element_type=jnp.float32)


def cache_kernel(n, head, sc, q_ref, *refs):
    k_parts, v_parts = part_refs(refs[: n + 1], n)
    acc_ref, m_ref, l_ref, kbuf, vbuf, vt_ref, s0, s1, t0, t1, sems = refs[n + 1 :]
    local = k_parts[0].shape[1]
    tiles, size, width = acc_ref.shape
    tokens = width // q_ref.shape[2]

    def copies(parts, buf, which):
        return [
            pltpu.make_async_copy(
                parts[i].at[head],
                buf.at[pl.ds(pl.multiple_of(sc[4 + i] * local, local), local)],
                sems.at[which, i],
            )
            for i in range(n)
        ]

    k_copies, v_copies = copies(k_parts, kbuf, 0), copies(v_parts, vbuf, 1)
    for copy in k_copies + v_copies:
        copy.start()
    m_ref[...] = jnp.full_like(m_ref, neg_large)
    l_ref[...] = jnp.zeros_like(l_ref)
    acc_ref[...] = jnp.zeros_like(acc_ref)
    for copy in v_copies:
        copy.wait()
    vt_ref[...] = vbuf[...].T
    for copy in k_copies:
        copy.wait()

    live = sc[1]
    chunks = pl.cdiv(live, cache_tile)

    def spot(chunk):
        return pl.ds(pl.multiple_of(chunk * cache_tile, cache_tile), cache_tile)

    def prepare(tile, chunk, s_ref, t_ref):
        q = q_ref[0, pl.ds(tile * tokens, tokens)].reshape(width, size)
        scores(q, kbuf[spot(chunk), :], s_ref, t_ref)

    def fix(tile, chunk, s_ref, t_ref):
        @pl.when((chunk + 1) * cache_tile > live)
        def _():
            hide(live - 1, chunk * cache_tile, s_ref, t_ref)

    def finish(tile, chunk, s_ref, t_ref):
        absorb(tile, vt_ref[:, spot(chunk)], s_ref, t_ref, m_ref, l_ref, acc_ref)

    def following(tile, chunk):
        last = chunk + 1 == chunks
        return jnp.where(last, jnp.minimum(tile + 1, tiles - 1), tile), jnp.where(last, 0, chunk + 1)

    start = (jnp.int32(0), jnp.int32(0))
    prepare(*start, s0, t0)
    fix(*start, s0, t0)

    def body(_, item):
        then = following(*item)
        prepare(*then, s1, t1)
        finish(*item, s0, t0)
        fix(*then, s1, t1)
        item = following(*then)
        prepare(*item, s0, t0)
        finish(*then, s1, t1)
        fix(*item, s0, t0)
        return item

    lax.fori_loop(0, tiles * chunks // 2, body, start)


def span_kernel(n, head, local_head, blocks, blk, sc, q_ref, acc_in, m_in, l_in, *refs):
    k_parts, v_parts = part_refs(refs[: n + 1], n)
    o_ref, kbuf, vbuf, vt_ref, s0, s1, t0, t1, m_ref, l_ref, acc_ref, work, sems = refs[-13:]
    rows = q_ref.shape[0]
    group, size = q_ref.shape[2:]
    width = blk * group
    per = blocks // n
    order = 4 + n

    def copies(r, parts, buf, which):
        out = []
        for i in range(n):
            for b in range(per):
                at = pl.multiple_of(sc[order + sc[4 + i] * per + b] * blk, blk)
                out.append(
                    pltpu.make_async_copy(
                        parts[i].at[r, local_head, pl.ds(b * blk, blk)],
                        buf.at[r, pl.ds(at, blk)],
                        sems.at[r, which, i * per + b],
                    )
                )
        return out

    k_copies = [c for r in range(rows) for c in copies(r, k_parts, kbuf, 0)]
    v_copies = [c for r in range(rows) for c in copies(r, v_parts, vbuf, 1)]
    for copy in k_copies + v_copies:
        copy.start()

    count = jnp.int32(0)
    for r in range(rows):
        live = sc[2 + r]
        for b in range(per):
            tile = r * per + b
            first = sc[order + sc[4] * per + b] * blk
            end = jnp.where(first < live, jnp.minimum(first + blk, live), 0)
            chunks = pl.cdiv(end, span_tile)

            def put(j, at, tile=tile, first=first, live=live, chunks=chunks):
                work[0, at] = tile
                work[1, at] = j
                work[2, at] = (j + 1 == chunks).astype(jnp.int32)
                work[3, at] = first
                work[4, at] = live - 1
                return at + 1

            count = lax.fori_loop(0, chunks, put, count)
    for extra in range(2):
        at = count + extra
        work[0, at] = work[0, jnp.maximum(count - 1, 0)] if extra == 0 else 0
        work[1, at] = 0
        work[2, at] = 1
        work[3, at] = 0
        work[4, at] = -1

    @pl.when(count == 0)
    def _():
        work[0, 0] = 0

    for r in range(rows):
        here = slice(r * per, (r + 1) * per)
        partial = sc[0] == r

        @pl.when(partial)
        def _(here=here):
            acc_ref[here] = acc_in[...]
            m_ref[here] = m_in[...]
            l_ref[here] = l_in[...]

        @pl.when(jnp.logical_not(partial))
        def _(here=here):
            acc_ref[here] = jnp.zeros((per, size, width), jnp.float32)
            m_ref[here] = jnp.full((per, 8, width), neg_large, jnp.float32)
            l_ref[here] = jnp.zeros((per, 8, width), jnp.float32)

    for copy in v_copies:
        copy.wait()
    for r in range(rows):
        vt_ref[r] = vbuf[r].T
    for copy in k_copies:
        copy.wait()

    def spot(at):
        return pl.ds(pl.multiple_of(work[1, at] * span_tile, span_tile), span_tile)

    def prepare(at, s_ref, t_ref):
        row, b = work[0, at] // per, work[0, at] % per
        q = q_ref[row, pl.ds(b * blk, blk)].reshape(width, size)
        scores(q, kbuf[row, spot(at), :], s_ref, t_ref)

    def fix(at, s_ref, t_ref):
        @pl.when(work[2, at] == 1)
        def _():
            token = work[3, at] + lax.broadcasted_iota(jnp.int32, (1, width), 1) // group
            hide(jnp.minimum(token, work[4, at]), work[1, at] * span_tile, s_ref, t_ref)

    def finish(at, s_ref, t_ref):
        row = work[0, at] // per
        absorb(work[0, at], vt_ref[row, :, spot(at)], s_ref, t_ref, m_ref, l_ref, acc_ref)

    prepare(0, s0, t0)
    fix(0, s0, t0)

    def body(i, _):
        prepare(2 * i + 1, s1, t1)
        finish(2 * i, s0, t0)
        fix(2 * i + 1, s1, t1)
        prepare(2 * i + 2, s0, t0)
        finish(2 * i + 1, s1, t1)
        fix(2 * i + 2, s0, t0)
        return 0

    lax.fori_loop(0, (count + 1) // 2, body, 0)

    for r in range(rows):
        for b in range(per):
            first = sc[order + sc[4] * per + b] * blk
            live = sc[2 + r]
            at = (r, slice(b * blk, (b + 1) * blk))

            @pl.when(first >= live)
            def _(at=at):
                o_ref[at] = jnp.zeros((blk, group, size), o_ref.dtype)

            @pl.when(first < live)
            def _(at=at, first=first, live=live, tile=r * per + b):
                total = over_sublanes(jnp.add, l_ref[tile])
                out = (acc_ref[tile].reshape(-1, 8, width) / total).reshape(size, width)
                query = lax.broadcasted_iota(jnp.int32, (1, width), 1)
                out = jnp.where(query < (live - first) * group, out, 0.0)
                o_ref[at] = out.astype(o_ref.dtype).T.reshape(blk, group, size)


def cache_call(scalars, q_rot, parts, head, blk):
    n = len(parts) - 1
    _, count, heads, size = q_rot.shape
    kv_heads, local, _ = parts[-1].shape
    group = heads // kv_heads
    slots = n * local
    tiles = count // blk
    width = blk * group
    pairs = count * group * slots
    state = lambda rows: jax.ShapeDtypeStruct((tiles, rows, width), jnp.float32)
    whole = lambda rows: pl.BlockSpec((tiles, rows, width), lambda i, sc: (0, 0, 0))
    return pl.pallas_call(
        functools.partial(cache_kernel, n, head),
        grid_spec=pltpu.PrefetchScalarGridSpec(
            num_scalar_prefetch=1,
            grid=(1,),
            in_specs=[pl.BlockSpec((1, count, group, size), lambda i, sc: (sc[0], 0, head, 0))]
            + [pl.BlockSpec(memory_space=pl.ANY)] * (n + 1),
            out_specs=[whole(size), whole(8), whole(8)],
            scratch_shapes=[
                pltpu.VMEM((slots, size), jnp.bfloat16),
                pltpu.VMEM((slots, size), jnp.bfloat16),
                pltpu.VMEM((size, slots), jnp.bfloat16),
                pltpu.VMEM((cache_tile, width), jnp.float32),
                pltpu.VMEM((cache_tile, width), jnp.float32),
                pltpu.VMEM((8, width), jnp.float32),
                pltpu.VMEM((8, width), jnp.float32),
                pltpu.SemaphoreType.DMA((2, n)),
            ],
        ),
        out_shape=[state(size), state(8), state(8)],
        compiler_params=pltpu.CompilerParams(
            vmem_limit_bytes=32 * 1024 * 1024
        ),
        cost_estimate=pl.CostEstimate(
            flops=pairs * size * 4, bytes_accessed=4 * 1024 * 1024, transcendentals=pairs
        ),
        name=f"cache_{head}",
    )(scalars, q_rot, *parts)


def span_call(scalars, q_rot, carry, parts, out, head, blocks, group):
    n = len(parts) - 1
    rows, count, heads, size = q_rot.shape
    _, unit_heads, local, _ = parts[-1].shape
    slots = n * local
    blk = slots // blocks
    width = blk * group
    per = blocks // n
    pairs = rows * count * group * slots
    whole = lambda depth: pl.BlockSpec((per, depth, width), lambda i, sc: (0, 0, 0))
    spot = pl.BlockSpec((rows, count, group, size), lambda i, sc: (0, 0, head, 0))
    items = rows * per * pl.cdiv(slots, span_tile) + 2
    first = out is None
    return pl.pallas_call(
        functools.partial(span_kernel, n, head, head % unit_heads, blocks, blk),
        grid_spec=pltpu.PrefetchScalarGridSpec(
            num_scalar_prefetch=1,
            grid=(1,),
            in_specs=[spot, whole(size), whole(8), whole(8)]
            + [pl.BlockSpec(memory_space=pl.ANY)] * (n + 1 + (not first)),
            out_specs=spot,
            scratch_shapes=[
                pltpu.VMEM((rows, slots, size), jnp.bfloat16),
                pltpu.VMEM((rows, slots, size), jnp.bfloat16),
                pltpu.VMEM((rows, size, slots), jnp.bfloat16),
                pltpu.VMEM((span_tile, width), jnp.float32),
                pltpu.VMEM((span_tile, width), jnp.float32),
                pltpu.VMEM((8, width), jnp.float32),
                pltpu.VMEM((8, width), jnp.float32),
                pltpu.VMEM((rows * per, 8, width), jnp.float32),
                pltpu.VMEM((rows * per, 8, width), jnp.float32),
                pltpu.VMEM((rows * per, size, width), jnp.float32),
                pltpu.SMEM((5, items), jnp.int32),
                pltpu.SemaphoreType.DMA((rows, 2, blocks)),
            ],
        ),
        out_shape=jax.ShapeDtypeStruct(q_rot.shape, q_rot.dtype),
        input_output_aliases={} if first else {6 + n: 0},
        compiler_params=pltpu.CompilerParams(
            vmem_limit_bytes=32 * 1024 * 1024
        ),
        cost_estimate=pl.CostEstimate(
            flops=pairs * size * 4, bytes_accessed=4 * 1024 * 1024, transcendentals=pairs
        ),
        name=f"span_{head}",
    )(scalars, q_rot, *carry, *parts, *([] if first else [out]))


def shards(
    ring,
    queries,
    span_key_rows,
    span_value_rows,
    prefix_key_rows,
    prefix_value_rows,
    cached_len,
    new_len,
    prefill_flag,
    block_order,
):
    n = len(ring)
    rows, count, heads, size = queries.shape
    kv_heads = span_key_rows.shape[2]
    group = heads // kv_heads
    blocks = block_order.shape[0]
    per = blocks // n
    blk = count // per
    ctx = lax.axis_index("ctx")

    partial = jnp.where(prefill_flag[0] == 0, 0, 1).astype(jnp.int32)
    cache = jnp.stack(
        [
            jnp.swapaxes(jnp.where(partial == 0, x[0], x[1]), 0, 1)
            for x in (prefix_key_rows, prefix_value_rows)
        ]
    )
    cache = ring_gather(cache, ring)

    half = size // 2
    mine = lax.dynamic_slice(block_order, (ctx * per,), (per,))
    q_index = (mine[:, None] * blk + jnp.arange(blk, dtype=jnp.int32)[None, :]).reshape(count)
    base = jnp.where(prefill_flag == 1, 0, cached_len)
    positions = base[:, None] + q_index[None, :]
    inverse = rope_base ** (-(jnp.arange(half, dtype=jnp.float32) * 2.0 / size))
    angle = positions.astype(jnp.float32)[:, :, None, None] * inverse
    cosine = jnp.cos(angle)
    sine = jnp.sin(angle)
    span = jnp.stack(
        [
            jnp.swapaxes(rotate(span_key_rows, cosine, sine), 1, 2),
            jnp.swapaxes(span_value_rows, 1, 2),
        ]
    )
    unit = -(-kv_heads // span_units)
    spans = [ring_gather(span[:, :, h : h + unit], ring) for h in range(0, kv_heads, unit)]
    q_rot = rotate(queries, cosine, sine)

    place = {c: i for i, c in enumerate(ring)}
    table = jnp.array(
        [[ring[(place[c] - s) % n] for s in range(n)] for c in range(n)], jnp.int32
    )
    sources = lax.dynamic_slice(table, (ctx, 0), (1, n)).reshape(n)
    live = jnp.where(partial == 0, cached_len[0], cached_len[1])
    scalars = jnp.concatenate([partial[None], live[None], new_len, sources, block_order])

    carries = [cache_call(scalars, q_rot, cache, h, blk) for h in range(kv_heads)]
    out = None
    for h in range(kv_heads):
        out = span_call(scalars, q_rot, carries[h], spans[h // unit], out, h, blocks, group)
    return out


def solution(mesh):
    ring = ring_order(mesh)
    return jax.shard_map(
        functools.partial(shards, ring),
        mesh=mesh,
        in_specs=(
            P("batch", "ctx", "tp", None),
            P("batch", "ctx", "tp", None),
            P("batch", "ctx", "tp", None),
            P("batch", "ctx", "tp", None),
            P("batch", "ctx", "tp", None),
            P("batch"),
            P("batch"),
            P("batch"),
            P(),
        ),
        out_specs=P("batch", "ctx", "tp", None),
        check_vma=False,
    )
```

```python
import functools

import jax
import jax.numpy as jnp
from jax import lax
from jax.experimental import pallas as pl
from jax.experimental.pallas import tpu as pltpu
from jax.sharding import PartitionSpec as P


rope_base = 500000.0
neg_large = -1e30
log2e = 1.4426950408889634
streams = 2
far = 1 << 29


def ring_order(mesh):
    n = mesh.shape["ctx"]
    plain = list(range(n))
    choices = [
        plain[0::2] + plain[1::2][::-1],
        plain[: n // 2] + plain[n // 2 :][::-1],
        plain,
    ]
    axis = mesh.axis_names.index("ctx")
    line = mesh.devices
    for k in reversed(range(line.ndim)):
        if k != axis:
            line = line.take(0, axis=k)

    def length(order):
        total = 0
        for a, b in zip(order, order[1:] + order[:1]):
            ca, cb = (getattr(line[i], "coords", (i,)) for i in (a, b))
            total += sum(abs(u - v) for u, v in zip(ca, cb))
        return total

    return min(choices, key=length)


def rotate(x, cosine, sine):
    half = x.shape[-1] // 2
    wide = x.astype(jnp.float32)
    first = wide[..., :half]
    second = wide[..., half:]
    return jnp.concatenate(
        [first * cosine - second * sine, second * cosine + first * sine], -1
    ).astype(jnp.bfloat16)


def over_sublanes(op, x):
    for shift in (4, 2, 1):
        x = op(x, pltpu.roll(x, shift, 0))
    return x


def largest(s, top_ref):
    top_ref[...] = over_sublanes(jnp.maximum, jnp.max(s.reshape(-1, 8, s.shape[1]), axis=0))


def scores(q, k, s_ref, top_ref):
    s = lax.dot_general(k, q, (((1,), (1,)), ((), ())), preferred_element_type=jnp.float32)
    s_ref[...] = s
    largest(s, top_ref)


def absorb(tile, vt, s_ref, top_ref, m_ref, l_ref, acc_ref):
    size, width = acc_ref.shape[1:]
    factor = log2e / size**0.5
    before = m_ref[tile]
    top = jnp.maximum(before, top_ref[...])
    alpha = jnp.exp2((before - top) * factor)
    prob = jnp.exp2(s_ref[...].reshape(-1, 8, width) * factor - top * factor)
    l_ref[tile] = l_ref[tile] * alpha + jnp.sum(prob, axis=0)
    m_ref[tile] = top
    prob = prob.reshape(s_ref.shape).astype(jnp.bfloat16)
    acc = (acc_ref[tile].reshape(-1, 8, width) * alpha).reshape(size, width)
    acc_ref[tile] = acc + jnp.dot(vt, prob, preferred_element_type=jnp.float32)


def hide(bound, bases, s_ref, top_ref):
    run = s_ref.shape[0] // len(bases)
    tops = []
    for i, base in enumerate(bases):
        key = base + lax.broadcasted_iota(jnp.int32, (run, s_ref.shape[1]), 0)
        s = jnp.where(key <= bound, s_ref[i * run : (i + 1) * run], neg_large)
        s_ref[i * run : (i + 1) * run] = s
        tops.append(jnp.max(s.reshape(-1, 8, s.shape[1]), axis=0))
    top_ref[...] = over_sublanes(jnp.maximum, functools.reduce(jnp.maximum, tops))


def step_kernel(cfg, sc, q_ref, *refs):
    n, blocks, blk, first_head, sources, packed, fresh, last, chained = cfg
    refs = list(refs)
    take = lambda k: [refs.pop(0) for _ in range(k)]
    carry = [] if fresh else take(3)
    if packed:
        pairs = [(ref.at[0], ref.at[1]) for ref in take(len(sources))]
    else:
        pairs = [tuple(take(2))]
    if chained:
        take(1)
    if last:
        (o_ref,) = take(1)
        acc_ref, m_ref, l_ref = refs[-3:]
        stage, o_sem = refs[-5:-3]
    else:
        acc_ref, m_ref, l_ref = take(3)
    kbuf, vt_ref, s0, s1, t0, t1, work = take(7)
    rows, count, _, size = q_ref.shape
    heads = pairs[0][0].shape[0]
    width = acc_ref.shape[2]
    group = width // blk
    per = blocks // n
    tiles = rows * per
    local = pairs[0][0].shape[1] - rows * count
    chunk = s0.shape[0]
    slots = kbuf.shape[0] // heads
    runs = chunk // blk
    order = 4 + n

    bases = []
    for h in range(heads):
        slot = h * slots
        for k_ref, v_ref in pairs:
            for c in range(local // chunk):
                kbuf[slot] = k_ref[h, c * chunk : (c + 1) * chunk]
                vt_ref[slot] = v_ref[h, c * chunk : (c + 1) * chunk].T
                slot += 1
        for r in range(rows):
            at = slice(local + r * count, local + (r + 1) * count)
            keys = [k_ref[h, at] for k_ref, _ in pairs]
            values = [v_ref[h, at] for _, v_ref in pairs]
            if len(pairs) * count < chunk:
                rest = jnp.zeros((chunk - len(pairs) * count, size), keys[0].dtype)
                keys.append(rest)
                values.append(rest)
            kbuf[slot] = jnp.concatenate(keys, 0)
            vt_ref[slot] = jnp.concatenate(values, 0).T
            slot += 1
    for i in sources:
        for c in range(local // chunk):
            bases.append([sc[4 + i] * local + c * chunk + run * blk for run in range(runs)])
    fresh_bases = [
        sc[order + sc[4 + i] * per + b] * blk for i in sources for b in range(per)
    ]
    fresh_bases += [jnp.int32(far)] * (runs - len(fresh_bases))
    bases += [fresh_bases] * rows
    for slot, base in enumerate(bases):
        for run in range(runs):
            work[5 + run, slot] = base[run]

    if fresh:
        acc_ref[...] = jnp.zeros_like(acc_ref)
        m_ref[...] = jnp.full_like(m_ref, neg_large)
        l_ref[...] = jnp.zeros_like(l_ref)
    else:
        acc_ref[...] = carry[0][...]
        m_ref[...] = carry[1][...]
        l_ref[...] = carry[2][...]

    def put(at, go, tile, slot, mask, first, limit):
        work[0, at] = tile
        work[1, at] = slot
        work[2, at] = mask.astype(jnp.int32)
        work[3, at] = first
        work[4, at] = limit
        return at + go.astype(jnp.int32)

    total = jnp.int32(0)
    for h in range(heads):
        for r in range(rows):
            live = sc[2 + r]
            for b in range(per):
                tile = (h * rows + r) * per + b
                first = sc[order + sc[4] * per + b] * blk
                alive = first < live
                for slot, base in enumerate(bases):
                    place = slot - (len(bases) - rows)
                    if place >= 0 and place != r:
                        continue
                    low = functools.reduce(jnp.minimum, base)
                    high = functools.reduce(jnp.maximum, base) + blk - 1
                    if place >= 0:
                        limit = live - 1
                        seen = low <= jnp.minimum(first + blk - 1, limit)
                        mask = high > jnp.minimum(first, limit)
                        total = put(total, alive & seen, tile, h * slots + slot, mask, first, limit)
                    else:
                        limit = sc[1] - 1
                        go = alive & (sc[0] == r) & (low <= limit)
                        total = put(total, go, tile, h * slots + slot, high > limit, jnp.int32(far), limit)
    work[0, total] = work[0, jnp.maximum(total - 1, 0)]
    for extra in range(2):
        if extra:
            work[0, total + extra] = 0
        work[1, total + extra] = 0
        work[2, total + extra] = 1
        work[3, total + extra] = 0
        work[4, total + extra] = -1

    def prepare(at, s_ref, t_ref):
        tile = work[0, at]
        h, r, b = tile // tiles, (tile // per) % rows, tile % per
        heads_at = pl.ds(pl.multiple_of((first_head + h) * group, group), group)
        q = q_ref[r, pl.ds(b * blk, blk), heads_at, :].reshape(width, size)
        scores(q, kbuf[work[1, at]], s_ref, t_ref)

    def fix(at, s_ref, t_ref):
        @pl.when(work[2, at] == 1)
        def _():
            slot = work[1, at] % slots
            token = work[3, at] + lax.broadcasted_iota(jnp.int32, (1, width), 1) // group
            bound = jnp.minimum(token, work[4, at])
            hide(bound, [work[5 + run, slot] for run in range(runs)], s_ref, t_ref)

    def finish(at, s_ref, t_ref):
        absorb(work[0, at], vt_ref[work[1, at]], s_ref, t_ref, m_ref, l_ref, acc_ref)

    @pl.when(total > 0)
    def _():
        prepare(0, s0, t0)
        fix(0, s0, t0)

    def body(i, _):
        prepare(2 * i + 1, s1, t1)
        finish(2 * i, s0, t0)
        fix(2 * i + 1, s1, t1)
        prepare(2 * i + 2, s0, t0)
        finish(2 * i + 1, s1, t1)
        fix(2 * i + 2, s0, t0)
        return 0

    lax.fori_loop(0, (total + 1) // 2, body, 0)

    if last:

        def write(tile):
            h, r, b = tile // tiles, (tile // per) % rows, tile % per
            heads_at = pl.ds(pl.multiple_of((first_head + h) * group, group), group)
            return pltpu.make_async_copy(
                stage.at[tile], o_ref.at[r, pl.ds(b * blk, blk), heads_at], o_sem.at[tile]
            )

        def store(tile, _):
            r, b = (tile // per) % rows, tile % per
            first = sc[order + sc[4] * per + b] * blk
            live = sc[2 + r]

            @pl.when(first >= live)
            def _():
                stage[tile] = jnp.zeros(stage.shape[1:], stage.dtype)

            @pl.when(first < live)
            def _():
                sums = over_sublanes(jnp.add, l_ref[tile])
                out = (acc_ref[tile].reshape(-1, 8, width) / sums).reshape(size, width)
                query = lax.broadcasted_iota(jnp.int32, (1, width), 1)
                out = jnp.where(query < (live - first) * group, out, 0.0)
                stage[tile] = out.astype(stage.dtype).T.reshape(stage.shape[1:])

            write(tile).start()
            return 0

        lax.fori_loop(0, heads * tiles, store, 0)
        lax.fori_loop(0, heads * tiles, lambda t, _: (write(t).wait(), 0)[1], 0)


def step_call(scalars, q_rot, carry, parts, sources, out, last, first_head, blocks, n, group):
    rows, count, _, size = q_rot.shape
    packed = parts[0].ndim == 4
    unit_heads, depth, _ = parts[0].shape[-3:]
    local = depth - rows * count
    per = blocks // n
    blk = count // per
    width = blk * group
    tiles = unit_heads * rows * per
    chunk = 2 * count
    slots = len(sources) * (local // chunk) + rows
    items = unit_heads * rows * per * (slots - rows + 1) + 2
    fresh, chained = carry is None, last and out is not None
    vmem, anywhere = pl.BlockSpec(memory_space=pltpu.VMEM), pl.BlockSpec(memory_space=pl.ANY)
    state = lambda d: (tiles, d, width)
    f32 = lambda d: jax.ShapeDtypeStruct(state(d), jnp.float32)
    scratch = [
        pltpu.VMEM((unit_heads * slots, chunk, size), jnp.bfloat16),
        pltpu.VMEM((unit_heads * slots, size, chunk), jnp.bfloat16),
        pltpu.VMEM((chunk, width), jnp.float32),
        pltpu.VMEM((chunk, width), jnp.float32),
        pltpu.VMEM((8, width), jnp.float32),
        pltpu.VMEM((8, width), jnp.float32),
        pltpu.SMEM((5 + chunk // blk, max(items, slots)), jnp.int32),
    ]
    operands = [scalars, q_rot] + ([] if fresh else list(carry)) + list(parts)
    specs = [pl.BlockSpec(memory_space=pltpu.SMEM)] + [vmem] * (len(operands) - 1)
    aliases = {} if fresh or last else {2: 0, 3: 1, 4: 2}
    if last:
        scratch += [
            pltpu.VMEM((tiles, blk, group, size), jnp.bfloat16),
            pltpu.SemaphoreType.DMA((tiles,)),
        ] + [pltpu.VMEM(state(d), jnp.float32) for d in (size, 8, 8)]
        if chained:
            operands.append(out)
            specs.append(anywhere)
            aliases = {len(operands) - 1: 0}
        shapes, out_specs = jax.ShapeDtypeStruct(q_rot.shape, q_rot.dtype), anywhere
    else:
        shapes, out_specs = [f32(size), f32(8), f32(8)], [vmem] * 3
    cfg = (n, blocks, blk, first_head, tuple(sources), packed, fresh, last, chained)
    pairs = items * chunk * width
    return pl.pallas_call(
        functools.partial(step_kernel, cfg),
        in_specs=specs,
        out_specs=out_specs,
        scratch_shapes=scratch,
        out_shape=shapes,
        input_output_aliases=aliases,
        compiler_params=pltpu.CompilerParams(vmem_limit_bytes=40 * 1024 * 1024),
        cost_estimate=pl.CostEstimate(
            flops=pairs * size * 4, bytes_accessed=1024 * 1024, transcendentals=pairs
        ),
        name=f"step_{first_head}_{sources[-1]}",
    )(*operands)


def shards(
    ring,
    queries,
    span_key_rows,
    span_value_rows,
    prefix_key_rows,
    prefix_value_rows,
    cached_len,
    new_len,
    prefill_flag,
    block_order,
):
    n = len(ring)
    rows, count, heads, size = queries.shape
    kv_heads = span_key_rows.shape[2]
    group = heads // kv_heads
    blocks = block_order.shape[0]
    per = blocks // n
    blk = count // per
    ctx = lax.axis_index("ctx")

    partial = jnp.where(prefill_flag[0] == 0, 0, 1).astype(jnp.int32)
    half = size // 2
    mine = lax.dynamic_slice(block_order, (ctx * per,), (per,))
    q_index = (mine[:, None] * blk + jnp.arange(blk, dtype=jnp.int32)[None, :]).reshape(count)
    base = jnp.where(prefill_flag == 1, 0, cached_len)
    positions = base[:, None] + q_index[None, :]
    inverse = rope_base ** (-(jnp.arange(half, dtype=jnp.float32) * 2.0 / size))
    angle = positions.astype(jnp.float32)[:, :, None, None] * inverse
    cosine = jnp.cos(angle)
    sine = jnp.sin(angle)
    unit = -(-kv_heads // streams)

    def payload(at):
        pick = lambda x: jnp.swapaxes(jnp.where(partial == 0, x[0], x[1])[:, at], 0, 1)
        new = lambda x: jnp.moveaxis(x, 2, 0).reshape(x.shape[2], rows * count, size)
        keys = new(rotate(span_key_rows[:, :, at], cosine, sine))
        values = new(span_value_rows[:, :, at])
        return jnp.stack(
            [
                jnp.concatenate([pick(prefix_key_rows), keys], 1),
                jnp.concatenate([pick(prefix_value_rows), values], 1),
            ]
        )

    q_rot = rotate(queries, cosine, sine)

    place = {c: i for i, c in enumerate(ring)}
    table = jnp.array(
        [[ring[(place[c] - s) % n] for s in range(n)] for c in range(n)], jnp.int32
    )
    sources = lax.dynamic_slice(table, (ctx, 0), (1, n)).reshape(n)
    live = jnp.where(partial == 0, cached_len[0], cached_len[1])
    scalars = jnp.concatenate([partial[None], live[None], new_len, sources, block_order])

    forward = [(ring[i], ring[(i + 1) % n]) for i in range(n)]
    backward = [(b, a) for a, b in forward]
    send = lambda x, way: lax.ppermute(x, "ctx", way)
    after = lambda x, y: lax.optimization_barrier((x, y))
    firsts = list(range(0, kv_heads, unit))
    own = [payload(slice(h, h + unit)) for h in firsts]
    ahead, back, carry = list(own), list(own), [None] * len(firsts)
    out = None

    def step(u, parts, sources, last=False):
        return step_call(
            scalars, q_rot, carry[u], parts, sources, out, last, firsts[u], blocks, n, group
        )

    for u in range(len(firsts)):
        ahead[u], back[u] = send(ahead[u], forward), send(back[u], backward)
    for u in range(len(firsts)):
        carry[u] = step(u, [own[u]], [0])
    for s in range(1, n // 2):
        for u in range(len(firsts)):
            here = [ahead[u], back[u]]
            if s + 1 < n // 2:
                ahead[u], back[u] = send(ahead[u], forward), send(back[u], backward)
            else:
                ahead[u], back[u] = send(ahead[u][0], forward), send(back[u][1], backward)
            carry[u] = step(u, here, [s, n - s])
            if s + 1 < n // 2:
                (ahead[u], back[u]), carry[u] = after((ahead[u], back[u]), carry[u])
    for u in range(len(firsts)):
        out = step(u, [ahead[u], back[u]], [n // 2], True)
    return out


def solution(mesh):
    ring = ring_order(mesh)
    return jax.shard_map(
        functools.partial(shards, ring),
        mesh=mesh,
        in_specs=(
            P("batch", "ctx", "tp", None),
            P("batch", "ctx", "tp", None),
            P("batch", "ctx", "tp", None),
            P("batch", "ctx", "tp", None),
            P("batch", "ctx", "tp", None),
            P("batch"),
            P("batch"),
            P("batch"),
            P(),
        ),
        out_specs=P("batch", "ctx", "tp", None),
        check_vma=False,
    )
```

```python
import functools

import jax
import jax.numpy as jnp
from jax import lax
from jax.experimental import pallas as pl
from jax.experimental.pallas import tpu as pltpu
from jax.sharding import PartitionSpec as P


rope_base = 500000.0
neg_large = -1e30
log2e = 1.4426950408889634
streams = 2
far = 1 << 29


def ring_order(mesh):
    n = mesh.shape["ctx"]
    plain = list(range(n))
    choices = [
        plain[0::2] + plain[1::2][::-1],
        plain[: n // 2] + plain[n // 2 :][::-1],
        plain,
    ]
    axis = mesh.axis_names.index("ctx")
    line = mesh.devices
    for k in reversed(range(line.ndim)):
        if k != axis:
            line = line.take(0, axis=k)

    def length(order):
        total = 0
        for a, b in zip(order, order[1:] + order[:1]):
            ca, cb = (getattr(line[i], "coords", (i,)) for i in (a, b))
            total += sum(abs(u - v) for u, v in zip(ca, cb))
        return total

    return min(choices, key=length)


def rotate(x, cosine, sine):
    half = x.shape[-1] // 2
    wide = x.astype(jnp.float32)
    first = wide[..., :half]
    second = wide[..., half:]
    return jnp.concatenate(
        [first * cosine - second * sine, second * cosine + first * sine], -1
    ).astype(jnp.bfloat16)


def over_sublanes(op, x):
    for shift in (4, 2, 1):
        x = op(x, pltpu.roll(x, shift, 0))
    return x


def largest(s, top_ref):
    top_ref[...] = over_sublanes(jnp.maximum, jnp.max(s.reshape(-1, 8, s.shape[1]), axis=0))


def scores(q, k, s_ref, top_ref):
    s = lax.dot_general(k, q, (((1,), (1,)), ((), ())), preferred_element_type=jnp.float32)
    s_ref[...] = s
    largest(s, top_ref)


def absorb(tile, vt, s_ref, top_ref, m_ref, l_ref, acc_ref):
    size, width = acc_ref.shape[1:]
    factor = log2e / size**0.5
    before = m_ref[tile]
    top = jnp.maximum(before, top_ref[...])
    alpha = jnp.exp2((before - top) * factor)
    prob = jnp.exp2(s_ref[...].reshape(-1, 8, width) * factor - top * factor)
    l_ref[tile] = l_ref[tile] * alpha + jnp.sum(prob, axis=0)
    m_ref[tile] = top
    prob = prob.reshape(s_ref.shape).astype(jnp.bfloat16)
    acc = (acc_ref[tile].reshape(-1, 8, width) * alpha).reshape(size, width)
    acc_ref[tile] = acc + jnp.dot(vt, prob, preferred_element_type=jnp.float32)


def hide(bound, bases, s_ref, top_ref):
    run = s_ref.shape[0] // len(bases)
    tops = []
    for i, base in enumerate(bases):
        key = base + lax.broadcasted_iota(jnp.int32, (run, s_ref.shape[1]), 0)
        s = jnp.where(key <= bound, s_ref[i * run : (i + 1) * run], neg_large)
        s_ref[i * run : (i + 1) * run] = s
        tops.append(jnp.max(s.reshape(-1, 8, s.shape[1]), axis=0))
    top_ref[...] = over_sublanes(jnp.maximum, functools.reduce(jnp.maximum, tops))


def step_kernel(cfg, sc, q_ref, *refs):
    n, blocks, blk, first_head, sources, packed, fresh, last, chained = cfg
    refs = list(refs)
    take = lambda k: [refs.pop(0) for _ in range(k)]
    carry = [] if fresh else take(3)
    if packed:
        pairs = [(ref.at[0], ref.at[1]) for ref in take(len(sources))]
    else:
        pairs = [tuple(take(2))]
    if chained:
        take(1)
    if last:
        (o_ref,) = take(1)
        acc_ref, m_ref, l_ref = refs[-3:]
        stage, o_sem = refs[-5:-3]
    else:
        acc_ref, m_ref, l_ref = take(3)
    kbuf, vt_ref, s0, s1, t0, t1, work = take(7)
    rows, count, _, size = q_ref.shape
    heads = pairs[0][0].shape[0]
    width = acc_ref.shape[2]
    group = width // blk
    per = blocks // n
    tiles = rows * per
    local = pairs[0][0].shape[1] - rows * count
    chunk = s0.shape[0]
    slots = kbuf.shape[0] // heads
    runs = chunk // blk
    order = 4 + n

    bases = []
    for h in range(heads):
        slot = h * slots
        for k_ref, v_ref in pairs:
            for c in range(local // chunk):
                kbuf[slot] = k_ref[h, c * chunk : (c + 1) * chunk]
                vt_ref[slot] = v_ref[h, c * chunk : (c + 1) * chunk].T
                slot += 1
        for r in range(rows):
            at = slice(local + r * count, local + (r + 1) * count)
            keys = [k_ref[h, at] for k_ref, _ in pairs]
            values = [v_ref[h, at] for _, v_ref in pairs]
            if len(pairs) * count < chunk:
                rest = jnp.zeros((chunk - len(pairs) * count, size), keys[0].dtype)
                keys.append(rest)
                values.append(rest)
            kbuf[slot] = jnp.concatenate(keys, 0)
            vt_ref[slot] = jnp.concatenate(values, 0).T
            slot += 1
    for i in sources:
        for c in range(local // chunk):
            bases.append([sc[4 + i] * local + c * chunk + run * blk for run in range(runs)])
    fresh_bases = [
        sc[order + sc[4 + i] * per + b] * blk for i in sources for b in range(per)
    ]
    fresh_bases += [jnp.int32(far)] * (runs - len(fresh_bases))
    bases += [fresh_bases] * rows
    for slot, base in enumerate(bases):
        for run in range(runs):
            work[5 + run, slot] = base[run]

    if fresh:
        acc_ref[...] = jnp.zeros_like(acc_ref)
        m_ref[...] = jnp.full_like(m_ref, neg_large)
        l_ref[...] = jnp.zeros_like(l_ref)
    else:
        acc_ref[...] = carry[0][...]
        m_ref[...] = carry[1][...]
        l_ref[...] = carry[2][...]

    def put(at, go, tile, slot, mask, first, limit):
        work[0, at] = tile
        work[1, at] = slot
        work[2, at] = mask.astype(jnp.int32)
        work[3, at] = first
        work[4, at] = limit
        return at + go.astype(jnp.int32)

    total = jnp.int32(0)
    for h in range(heads):
        for r in range(rows):
            live = sc[2 + r]
            for b in range(per):
                tile = (h * rows + r) * per + b
                first = sc[order + sc[4] * per + b] * blk
                alive = first < live
                for slot, base in enumerate(bases):
                    place = slot - (len(bases) - rows)
                    if place >= 0 and place != r:
                        continue
                    low = functools.reduce(jnp.minimum, base)
                    high = functools.reduce(jnp.maximum, base) + blk - 1
                    if place >= 0:
                        limit = live - 1
                        seen = low <= jnp.minimum(first + blk - 1, limit)
                        mask = high > jnp.minimum(first, limit)
                        total = put(total, alive & seen, tile, h * slots + slot, mask, first, limit)
                    else:
                        limit = sc[1] - 1
                        go = alive & (sc[0] == r) & (low <= limit)
                        total = put(total, go, tile, h * slots + slot, high > limit, jnp.int32(far), limit)
    work[0, total] = work[0, jnp.maximum(total - 1, 0)]
    for extra in range(2):
        if extra:
            work[0, total + extra] = 0
        work[1, total + extra] = 0
        work[2, total + extra] = 1
        work[3, total + extra] = 0
        work[4, total + extra] = -1

    def prepare(at, s_ref, t_ref):
        tile = work[0, at]
        h, r, b = tile // tiles, (tile // per) % rows, tile % per
        heads_at = pl.ds(pl.multiple_of((first_head + h) * group, group), group)
        q = q_ref[r, pl.ds(b * blk, blk), heads_at, :].reshape(width, size)
        scores(q, kbuf[work[1, at]], s_ref, t_ref)

    def fix(at, s_ref, t_ref):
        @pl.when(work[2, at] == 1)
        def _():
            slot = work[1, at] % slots
            token = work[3, at] + lax.broadcasted_iota(jnp.int32, (1, width), 1) // group
            bound = jnp.minimum(token, work[4, at])
            hide(bound, [work[5 + run, slot] for run in range(runs)], s_ref, t_ref)

    def finish(at, s_ref, t_ref):
        absorb(work[0, at], vt_ref[work[1, at]], s_ref, t_ref, m_ref, l_ref, acc_ref)

    @pl.when(total > 0)
    def _():
        prepare(0, s0, t0)
        fix(0, s0, t0)

    def body(i, _):
        prepare(2 * i + 1, s1, t1)
        finish(2 * i, s0, t0)
        fix(2 * i + 1, s1, t1)
        prepare(2 * i + 2, s0, t0)
        finish(2 * i + 1, s1, t1)
        fix(2 * i + 2, s0, t0)
        return 0

    lax.fori_loop(0, (total + 1) // 2, body, 0)

    if last:

        def write(tile):
            h, r, b = tile // tiles, (tile // per) % rows, tile % per
            heads_at = pl.ds(pl.multiple_of((first_head + h) * group, group), group)
            return pltpu.make_async_copy(
                stage.at[tile], o_ref.at[r, pl.ds(b * blk, blk), heads_at], o_sem.at[tile]
            )

        def store(tile, _):
            r, b = (tile // per) % rows, tile % per
            first = sc[order + sc[4] * per + b] * blk
            live = sc[2 + r]

            @pl.when(first >= live)
            def _():
                stage[tile] = jnp.zeros(stage.shape[1:], stage.dtype)

            @pl.when(first < live)
            def _():
                sums = over_sublanes(jnp.add, l_ref[tile])
                out = (acc_ref[tile].reshape(-1, 8, width) / sums).reshape(size, width)
                query = lax.broadcasted_iota(jnp.int32, (1, width), 1)
                out = jnp.where(query < (live - first) * group, out, 0.0)
                stage[tile] = out.astype(stage.dtype).T.reshape(stage.shape[1:])

            write(tile).start()
            return 0

        lax.fori_loop(0, heads * tiles, store, 0)
        lax.fori_loop(0, heads * tiles, lambda t, _: (write(t).wait(), 0)[1], 0)


def step_call(scalars, q_rot, carry, parts, sources, out, last, first_head, blocks, n, group):
    rows, count, _, size = q_rot.shape
    packed = parts[0].ndim == 4
    unit_heads, depth, _ = parts[0].shape[-3:]
    local = depth - rows * count
    per = blocks // n
    blk = count // per
    width = blk * group
    tiles = unit_heads * rows * per
    chunk = 2 * count
    slots = len(sources) * (local // chunk) + rows
    items = unit_heads * rows * per * (slots - rows + 1) + 2
    fresh, chained = carry is None, last and out is not None
    vmem, anywhere = pl.BlockSpec(memory_space=pltpu.VMEM), pl.BlockSpec(memory_space=pl.ANY)
    state = lambda d: (tiles, d, width)
    f32 = lambda d: jax.ShapeDtypeStruct(state(d), jnp.float32)
    scratch = [
        pltpu.VMEM((unit_heads * slots, chunk, size), jnp.bfloat16),
        pltpu.VMEM((unit_heads * slots, size, chunk), jnp.bfloat16),
        pltpu.VMEM((chunk, width), jnp.float32),
        pltpu.VMEM((chunk, width), jnp.float32),
        pltpu.VMEM((8, width), jnp.float32),
        pltpu.VMEM((8, width), jnp.float32),
        pltpu.SMEM((5 + chunk // blk, max(items, slots)), jnp.int32),
    ]
    operands = [scalars, q_rot] + ([] if fresh else list(carry)) + list(parts)
    specs = [pl.BlockSpec(memory_space=pltpu.SMEM)] + [vmem] * (len(operands) - 1)
    aliases = {} if fresh or last else {2: 0, 3: 1, 4: 2}
    if last:
        scratch += [
            pltpu.VMEM((tiles, blk, group, size), jnp.bfloat16),
            pltpu.SemaphoreType.DMA((tiles,)),
        ] + [pltpu.VMEM(state(d), jnp.float32) for d in (size, 8, 8)]
        if chained:
            operands.append(out)
            specs.append(anywhere)
            aliases = {len(operands) - 1: 0}
        shapes, out_specs = jax.ShapeDtypeStruct(q_rot.shape, q_rot.dtype), anywhere
    else:
        shapes, out_specs = [f32(size), f32(8), f32(8)], [vmem] * 3
    cfg = (n, blocks, blk, first_head, tuple(sources), packed, fresh, last, chained)
    pairs = items * chunk * width
    return pl.pallas_call(
        functools.partial(step_kernel, cfg),
        in_specs=specs,
        out_specs=out_specs,
        scratch_shapes=scratch,
        out_shape=shapes,
        input_output_aliases=aliases,
        compiler_params=pltpu.CompilerParams(vmem_limit_bytes=24 * 1024 * 1024),
        cost_estimate=pl.CostEstimate(
            flops=pairs * size * 4, bytes_accessed=1024 * 1024, transcendentals=pairs
        ),
    )(*operands)


def turn_kernel(parts, q_ref, cosine_ref, sine_ref, o_ref):
    i = pl.program_id(0)
    tokens, _, size = q_ref.shape[1:]
    x = q_ref[0].astype(jnp.float32)
    cosine = cosine_ref[0][:, None, :]
    sine = sine_ref[0][:, None, :]
    turned = x * cosine + pltpu.roll(x, size // 2, 2) * sine
    at = pl.ds(pl.multiple_of((i % parts) * tokens, tokens), tokens)
    o_ref[i // parts, at] = turned.astype(o_ref.dtype)


def turn_call(queries, cosine, sine):
    rows, count, heads, size = queries.shape
    tokens = 16
    parts = count // tokens
    table = pl.BlockSpec((1, tokens, size), lambda i: (i // parts, i % parts, 0))
    return pl.pallas_call(
        functools.partial(turn_kernel, parts),
        grid=(rows * parts,),
        in_specs=[
            pl.BlockSpec((1, tokens, heads, size), lambda i: (i // parts, i % parts, 0, 0)),
            table,
            table,
        ],
        out_specs=pl.BlockSpec(queries.shape, lambda i: (0, 0, 0, 0)),
        out_shape=jax.ShapeDtypeStruct(queries.shape, queries.dtype),
        compiler_params=pltpu.CompilerParams(vmem_limit_bytes=16 * 1024 * 1024),
        cost_estimate=pl.CostEstimate(
            flops=queries.size * 4, bytes_accessed=queries.size * 4, transcendentals=0
        ),
        name="turn",
    )(queries, cosine, sine)


def shards(
    ring,
    queries,
    span_key_rows,
    span_value_rows,
    prefix_key_rows,
    prefix_value_rows,
    cached_len,
    new_len,
    prefill_flag,
    block_order,
):
    n = len(ring)
    rows, count, heads, size = queries.shape
    kv_heads = span_key_rows.shape[2]
    group = heads // kv_heads
    blocks = block_order.shape[0]
    per = blocks // n
    blk = count // per
    ctx = lax.axis_index("ctx")

    partial = jnp.where(prefill_flag[0] == 0, 0, 1).astype(jnp.int32)
    half = size // 2
    mine = lax.dynamic_slice(block_order, (ctx * per,), (per,))
    q_index = (mine[:, None] * blk + jnp.arange(blk, dtype=jnp.int32)[None, :]).reshape(count)
    base = jnp.where(prefill_flag == 1, 0, cached_len)
    positions = base[:, None] + q_index[None, :]
    inverse = rope_base ** (-(jnp.arange(half, dtype=jnp.float32) * 2.0 / size))
    angle = positions.astype(jnp.float32)[:, :, None, None] * inverse
    cosine = jnp.cos(angle)
    sine = jnp.sin(angle)
    unit = -(-kv_heads // streams)

    def payload(at):
        pick = lambda x: jnp.swapaxes(jnp.where(partial == 0, x[0], x[1])[:, at], 0, 1)
        new = lambda x: jnp.moveaxis(x, 2, 0).reshape(x.shape[2], rows * count, size)
        keys = new(rotate(span_key_rows[:, :, at], cosine, sine))
        values = new(span_value_rows[:, :, at])
        return jnp.stack(
            [
                jnp.concatenate([pick(prefix_key_rows), keys], 1),
                jnp.concatenate([pick(prefix_value_rows), values], 1),
            ]
        )

    both = lambda x, y: jnp.concatenate([x[:, :, 0], y[:, :, 0]], -1)
    q_rot = turn_call(queries, both(cosine, cosine), both(-sine, sine))

    place = {c: i for i, c in enumerate(ring)}
    table = jnp.array(
        [[ring[(place[c] - s) % n] for s in range(n)] for c in range(n)], jnp.int32
    )
    sources = lax.dynamic_slice(table, (ctx, 0), (1, n)).reshape(n)
    live = jnp.where(partial == 0, cached_len[0], cached_len[1])
    scalars = jnp.concatenate([partial[None], live[None], new_len, sources, block_order])

    forward = [(ring[i], ring[(i + 1) % n]) for i in range(n)]
    backward = [(b, a) for a, b in forward]

    def send(x, way):
        return lax.ppermute(x, "ctx", way)

    firsts = list(range(0, kv_heads, unit))
    count_u = len(firsts)
    own = [payload(slice(h, h + unit)) for h in firsts]
    ahead, back, carry = list(own), list(own), [None] * count_u
    out = None

    def step(todo, tied=None, last=False):
        u, parts, sources = todo
        return step_call(
            scalars if tied is None else tied,
            q_rot,
            carry[u],
            parts,
            sources,
            out,
            last,
            firsts[u],
            blocks,
            n,
            group,
        )

    for u in range(count_u):
        ahead[u], back[u] = send(ahead[u], forward), send(back[u], backward)
    carry[0] = step((0, [own[0]], [0]))
    waiting = [(u, [own[u]], [0]) for u in range(1, count_u)]
    for s in range(1, n // 2):
        for u in range(count_u):
            here, there, tied = lax.optimization_barrier((ahead[u], back[u], scalars))
            waiting.append((u, [here, there], [s, n - s]))
            if s + 1 == n // 2:
                here, there = here[0], there[1]
            if carry[u] is not None:
                here, there, carry[u] = lax.optimization_barrier((here, there, carry[u]))
            ahead[u], back[u] = send(here, forward), send(there, backward)
            todo = waiting.pop(0)
            carry[todo[0]] = step(todo, tied)
    for todo in waiting:
        carry[todo[0]] = step(todo)
    for u in range(count_u):
        out = step((u, [ahead[u], back[u]], [n // 2]), last=True)
    return out


def solution(mesh):
    ring = ring_order(mesh)
    return jax.shard_map(
        functools.partial(shards, ring),
        mesh=mesh,
        in_specs=(
            P("batch", "ctx", "tp", None),
            P("batch", "ctx", "tp", None),
            P("batch", "ctx", "tp", None),
            P("batch", "ctx", "tp", None),
            P("batch", "ctx", "tp", None),
            P("batch"),
            P("batch"),
            P("batch"),
            P(),
        ),
        out_specs=P("batch", "ctx", "tp", None),
        check_vma=False,
    )
```

```python
import functools

import jax
import jax.numpy as jnp
from jax import lax
from jax.experimental import pallas as pl
from jax.experimental.pallas import tpu as pltpu
from jax.sharding import PartitionSpec as P


rope_base = 500000.0
neg_large = -1e30
log2e = 1.4426950408889634
streams = 2
chunk_units = 4
far = 1 << 29


def ring_order(mesh):
    n = mesh.shape["ctx"]
    plain = list(range(n))
    choices = [
        plain[0::2] + plain[1::2][::-1],
        plain[: n // 2] + plain[n // 2 :][::-1],
        plain,
    ]
    axis = mesh.axis_names.index("ctx")
    line = mesh.devices
    for k in reversed(range(line.ndim)):
        if k != axis:
            line = line.take(0, axis=k)

    def length(order):
        total = 0
        for a, b in zip(order, order[1:] + order[:1]):
            ca, cb = (getattr(line[i], "coords", (i,)) for i in (a, b))
            total += sum(abs(u - v) for u, v in zip(ca, cb))
        return total

    return min(choices, key=length)


def rotate(x, cosine, sine):
    half = x.shape[-1] // 2
    wide = x.astype(jnp.float32)
    first = wide[..., :half]
    second = wide[..., half:]
    return jnp.concatenate(
        [first * cosine - second * sine, second * cosine + first * sine], -1
    ).astype(jnp.bfloat16)


def over_sublanes(op, x):
    for shift in (4, 2, 1):
        x = op(x, pltpu.roll(x, shift, 0))
    return x


def largest(s, top_ref):
    top_ref[...] = over_sublanes(jnp.maximum, jnp.max(s.reshape(-1, 8, s.shape[1]), axis=0))


def scores(q, k, s_ref, top_ref):
    s = lax.dot_general(k, q, (((1,), (1,)), ((), ())), preferred_element_type=jnp.float32)
    s_ref[...] = s
    largest(s, top_ref)


def absorb(tile, vt, s_ref, top_ref, m_ref, l_ref, acc_ref):
    size, width = acc_ref.shape[1:]
    factor = log2e / size**0.5
    before = m_ref[tile]
    top = jnp.maximum(before, top_ref[...])
    alpha = jnp.exp2((before - top) * factor)
    prob = jnp.exp2(s_ref[...].reshape(-1, 8, width) * factor - top * factor)
    l_ref[tile] = l_ref[tile] * alpha + jnp.sum(prob, axis=0)
    m_ref[tile] = top
    prob = prob.reshape(s_ref.shape).astype(jnp.bfloat16)
    acc = (acc_ref[tile].reshape(-1, 8, width) * alpha).reshape(size, width)
    acc_ref[tile] = acc + jnp.dot(vt, prob, preferred_element_type=jnp.float32)


def hide(token, runs, s_ref, top_ref):
    size = s_ref.shape[0] // len(runs)
    tops = []
    for i, (base, offset, limit) in enumerate(runs):
        bound = jnp.minimum(token + offset, limit) - base
        key = lax.broadcasted_iota(jnp.int32, (size, s_ref.shape[1]), 0)
        s = jnp.where(key <= bound, s_ref[i * size : (i + 1) * size], neg_large)
        s_ref[i * size : (i + 1) * size] = s
        tops.append(jnp.max(s.reshape(-1, 8, s.shape[1]), axis=0))
    top_ref[...] = over_sublanes(jnp.maximum, functools.reduce(jnp.maximum, tops))


def plan(n, cache_units):
    half = n // 2
    steps, partial, prefill = [], [], []
    for s in range(1, half + 1):
        arrived = [s, n - s] if s < half else [half]
        for source in ([0] if s == 1 else []) + arrived:
            partial += [(source, c) for c in range(cache_units)] + [(source, None)]
            prefill += [(source, None)]
        chunks = []
        for kind, queue in ((0, partial), (1, prefill)):
            while len(queue) >= chunk_units or (s == half and queue):
                chunks.append((kind, tuple(queue[:chunk_units])))
                del queue[:chunk_units]
        steps.append(chunks)
    return steps


def step_kernel(cfg, sc, q_ref, *refs):
    n, blocks, blk, first_head, chunks, sources, packed, fresh, last, chained = cfg
    refs = list(refs)
    take = lambda k: [refs.pop(0) for _ in range(k)]
    carry = [] if fresh else take(3)
    pairs = {}
    for source, one in zip(sources, packed):
        if one:
            (ref,) = take(1)
            pairs[source] = (ref.at[0], ref.at[1])
        else:
            pairs[source] = tuple(take(2))
    if chained:
        take(1)
    if last:
        (o_ref,) = take(1)
        acc_ref, m_ref, l_ref = refs[-3:]
        stage, o_sem = refs[-5:-3]
    else:
        acc_ref, m_ref, l_ref = take(3)
    kbuf, vt_ref, qbuf, s0, s1, t0, t1, work, q_sem = take(9)
    rows, count, _, size = q_ref.shape
    heads = pairs[sources[0]][0].shape[0]
    width = acc_ref.shape[2]
    group = width // blk
    per = blocks // n
    tiles = rows * per
    local = pairs[sources[0]][0].shape[1] - rows * count
    runs = s0.shape[0] // blk
    order = 4 + n
    row_of = lambda kind: sc[0] if kind == 0 else 1 - sc[0]
    run_at = 5

    def fetch(tile):
        h, r, b = tile // tiles, (tile // per) % rows, tile % per
        heads_at = pl.ds((first_head + h) * group, group)
        return pltpu.make_async_copy(
            q_ref.at[r, pl.ds(b * blk, blk), heads_at], qbuf.at[tile], q_sem.at[tile]
        )

    for tile in range(heads * tiles):
        fetch(tile).start()

    for i, (kind, units) in enumerate(chunks):
        row = row_of(kind)
        live = sc[2 + row]
        table = []
        for h in range(heads):
            keys, values = [], []
            for source, c in units:
                k_ref, v_ref = pairs[source]
                start = local + row * count if c is None else c * count
                at = pl.ds(start if c is not None else pl.multiple_of(start, count), count)
                keys.append(k_ref[h, at])
                values.append(v_ref[h, at])
            rest = s0.shape[0] - len(units) * count
            if rest:
                keys.append(jnp.zeros((rest, size), keys[0].dtype))
                values.append(jnp.zeros((rest, size), keys[0].dtype))
            kbuf[h * len(chunks) + i] = jnp.concatenate(keys, 0)
            vt_ref[h * len(chunks) + i] = jnp.concatenate(values, 0).T
        for source, c in units:
            for b in range(per):
                if c is None:
                    table.append((sc[order + sc[4 + source] * per + b] * blk, 0, live - 1))
                else:
                    table.append((sc[4 + source] * local + c * count + b * blk, far, sc[1] - 1))
        table += [(0, 0, -1)] * (runs - len(table))
        for run, entry in enumerate(table):
            for j, value in enumerate(entry):
                work[run_at + 3 * run + j, i] = value

    if fresh:
        acc_ref[...] = jnp.zeros_like(acc_ref)
        m_ref[...] = jnp.full_like(m_ref, neg_large)
        l_ref[...] = jnp.zeros_like(l_ref)
    else:
        acc_ref[...] = carry[0][...]
        m_ref[...] = carry[1][...]
        l_ref[...] = carry[2][...]

    total = jnp.int32(0)
    for i, (kind, _) in enumerate(chunks):
        row = row_of(kind)
        for b in range(per):
            first = sc[order + sc[4] * per + b] * blk

            def look(run, state, first=first, i=i):
                seen, hidden = state
                base, offset, limit = (work[run_at + 3 * run + j, i] for j in range(3))
                least = jnp.minimum(first + offset, limit)
                most = jnp.minimum(first + blk - 1 + offset, limit)
                seen = seen | (base <= most).astype(jnp.int32)
                return seen, hidden | (base + blk - 1 > least).astype(jnp.int32)

            state = (jnp.int32(0), jnp.int32(0))
            for run in range(runs):
                state = look(run, state)
            go = jnp.where(first < sc[2 + row], state[0], 0)
            for h in range(heads):
                work[0, total] = (h * rows + row) * per + b
                work[1, total] = h * len(chunks) + i
                work[2, total] = state[1]
                work[3, total] = first
                work[4, total] = i
                total = total + go
    none = len(chunks)
    for run in range(runs):
        for j, value in enumerate((0, 0, -1)):
            work[run_at + 3 * run + j, none] = value
    work[0, total] = work[0, jnp.maximum(total - 1, 0)]
    work[0, total + 1] = 0
    for extra in range(2):
        work[1, total + extra] = 0
        work[2, total + extra] = 1
        work[3, total + extra] = 0
        work[4, total + extra] = none

    def prepare(at, s_ref, t_ref):
        q = qbuf[work[0, at]].reshape(width, size)
        scores(q, kbuf[work[1, at]], s_ref, t_ref)

    def fix(at, s_ref, t_ref):
        @pl.when(work[2, at] == 1)
        def _():
            i = work[4, at]
            token = work[3, at] + lax.broadcasted_iota(jnp.int32, (1, width), 1) // group
            table = [[work[run_at + 3 * run + j, i] for j in range(3)] for run in range(runs)]
            hide(token, table, s_ref, t_ref)

    def finish(at, s_ref, t_ref):
        absorb(work[0, at], vt_ref[work[1, at]], s_ref, t_ref, m_ref, l_ref, acc_ref)

    for tile in range(heads * tiles):
        fetch(tile).wait()

    @pl.when(total > 0)
    def _():
        prepare(0, s0, t0)
        fix(0, s0, t0)

    def body(i, _):
        prepare(2 * i + 1, s1, t1)
        finish(2 * i, s0, t0)
        fix(2 * i + 1, s1, t1)
        prepare(2 * i + 2, s0, t0)
        finish(2 * i + 1, s1, t1)
        fix(2 * i + 2, s0, t0)
        return 0

    lax.fori_loop(0, (total + 1) // 2, body, 0)

    if last:

        def write(tile):
            h, r, b = tile // tiles, (tile // per) % rows, tile % per
            heads_at = pl.ds(pl.multiple_of((first_head + h) * group, group), group)
            return pltpu.make_async_copy(
                stage.at[tile], o_ref.at[r, pl.ds(b * blk, blk), heads_at], o_sem.at[tile]
            )

        def store(tile, _):
            r, b = (tile // per) % rows, tile % per
            first = sc[order + sc[4] * per + b] * blk
            live = sc[2 + r]

            @pl.when(first >= live)
            def _():
                stage[tile] = jnp.zeros(stage.shape[1:], stage.dtype)

            @pl.when(first < live)
            def _():
                sums = over_sublanes(jnp.add, l_ref[tile])
                out = (acc_ref[tile].reshape(-1, 8, width) / sums).reshape(size, width)
                query = lax.broadcasted_iota(jnp.int32, (1, width), 1)
                out = jnp.where(query < (live - first) * group, out, 0.0)
                stage[tile] = out.astype(stage.dtype).T.reshape(stage.shape[1:])

            write(tile).start()
            return 0

        lax.fori_loop(0, heads * tiles, store, 0)
        lax.fori_loop(0, heads * tiles, lambda t, _: (write(t).wait(), 0)[1], 0)


def step_call(scalars, q_rot, carry, parts, chunks, out, last, first_head, blocks, n, group):
    rows, count, _, size = q_rot.shape
    sources = sorted({source for _, units in chunks for source, _ in units})
    packed = tuple(not isinstance(parts[source], tuple) for source in sources)
    arrays = []
    for source in sources:
        arrays += list(parts[source]) if isinstance(parts[source], tuple) else [parts[source]]
    unit_heads = arrays[0].shape[-3]
    per = blocks // n
    blk = count // per
    width = blk * group
    tiles = unit_heads * rows * per
    depth = chunk_units * count
    items = unit_heads * per * len(chunks)
    fresh, chained = carry is None, last and out is not None
    vmem, anywhere = pl.BlockSpec(memory_space=pltpu.VMEM), pl.BlockSpec(memory_space=pl.ANY)
    state = lambda d: (tiles, d, width)
    f32 = lambda d: jax.ShapeDtypeStruct(state(d), jnp.float32)
    scratch = [
        pltpu.VMEM((unit_heads * len(chunks), depth, size), jnp.bfloat16),
        pltpu.VMEM((unit_heads * len(chunks), size, depth), jnp.bfloat16),
        pltpu.VMEM((tiles, blk, group, size), jnp.bfloat16),
        pltpu.VMEM((depth, width), jnp.float32),
        pltpu.VMEM((depth, width), jnp.float32),
        pltpu.VMEM((8, width), jnp.float32),
        pltpu.VMEM((8, width), jnp.float32),
        pltpu.SMEM((5 + 3 * depth // blk, items + 2), jnp.int32),
        pltpu.SemaphoreType.DMA((tiles,)),
    ]
    q_rot = pltpu.with_memory_space_constraint(q_rot, pltpu.HBM)
    operands = [scalars, q_rot] + ([] if fresh else list(carry)) + arrays
    specs = [pl.BlockSpec(memory_space=pltpu.SMEM), pl.BlockSpec(memory_space=pltpu.HBM)] + [vmem] * (len(operands) - 2)
    aliases = {} if fresh or last else {2: 0, 3: 1, 4: 2}
    if last:
        scratch += [
            pltpu.VMEM((tiles, blk, group, size), jnp.bfloat16),
            pltpu.SemaphoreType.DMA((tiles,)),
        ] + [pltpu.VMEM(state(d), jnp.float32) for d in (size, 8, 8)]
        if chained:
            operands.append(out)
            specs.append(anywhere)
            aliases = {len(operands) - 1: 0}
        shapes, out_specs = jax.ShapeDtypeStruct(q_rot.shape, q_rot.dtype), anywhere
    else:
        shapes, out_specs = [f32(size), f32(8), f32(8)], [vmem] * 3
    cfg = (n, blocks, blk, first_head, chunks, sources, packed, fresh, last, chained)
    pairs = items * depth * width
    return pl.pallas_call(
        functools.partial(step_kernel, cfg),
        in_specs=specs,
        out_specs=out_specs,
        scratch_shapes=scratch,
        out_shape=shapes,
        input_output_aliases=aliases,
        compiler_params=pltpu.CompilerParams(vmem_limit_bytes=(20 if last else 14) * 1024 * 1024),
        cost_estimate=pl.CostEstimate(
            flops=pairs * size * 4, bytes_accessed=1024 * 1024, transcendentals=pairs
        ),
    )(*operands)


def turn_kernel(q_ref, cosine_ref, sine_ref, o_ref):
    size = q_ref.shape[-1]
    x = q_ref[0].astype(jnp.float32)
    cosine = cosine_ref[0][:, None, :]
    sine = sine_ref[0][:, None, :]
    turned = x * cosine + pltpu.roll(x, size // 2, 2) * sine
    o_ref[0] = turned.astype(o_ref.dtype)


def turn_call(queries, cosine, sine):
    rows, count, heads, size = queries.shape
    tokens = 16
    parts = count // tokens
    table = pl.BlockSpec((1, tokens, size), lambda i: (i // parts, i % parts, 0))
    spot = pl.BlockSpec((1, tokens, heads, size), lambda i: (i // parts, i % parts, 0, 0))
    return pl.pallas_call(
        turn_kernel,
        grid=(rows * parts,),
        in_specs=[spot, table, table],
        out_specs=spot,
        out_shape=pltpu.HBM(queries.shape, queries.dtype),
        compiler_params=pltpu.CompilerParams(vmem_limit_bytes=8 * 1024 * 1024),
        cost_estimate=pl.CostEstimate(
            flops=queries.size * 4, bytes_accessed=queries.size * 4, transcendentals=0
        ),
        name="turn",
    )(pltpu.with_memory_space_constraint(queries, pltpu.HBM), cosine, sine)


def shards(
    ring,
    queries,
    span_key_rows,
    span_value_rows,
    prefix_key_rows,
    prefix_value_rows,
    cached_len,
    new_len,
    prefill_flag,
    block_order,
):
    n = len(ring)
    rows, count, heads, size = queries.shape
    kv_heads = span_key_rows.shape[2]
    group = heads // kv_heads
    blocks = block_order.shape[0]
    per = blocks // n
    blk = count // per
    ctx = lax.axis_index("ctx")

    partial = jnp.where(prefill_flag[0] == 0, 0, 1).astype(jnp.int32)
    half = size // 2
    mine = lax.dynamic_slice(block_order, (ctx * per,), (per,))
    q_index = (mine[:, None] * blk + jnp.arange(blk, dtype=jnp.int32)[None, :]).reshape(count)
    base = jnp.where(prefill_flag == 1, 0, cached_len)
    positions = base[:, None] + q_index[None, :]
    inverse = rope_base ** (-(jnp.arange(half, dtype=jnp.float32) * 2.0 / size))
    angle = positions.astype(jnp.float32)[:, :, None, None] * inverse
    cosine = jnp.cos(angle)
    sine = jnp.sin(angle)
    unit = -(-kv_heads // streams)

    def payload(at):
        pick = lambda x: jnp.swapaxes(jnp.where(partial == 0, x[0], x[1])[:, at], 0, 1)
        new = lambda x: jnp.moveaxis(x, 2, 0).reshape(x.shape[2], rows * count, size)
        keys = new(rotate(span_key_rows[:, :, at], cosine, sine))
        values = new(span_value_rows[:, :, at])
        return jnp.stack(
            [
                jnp.concatenate([pick(prefix_key_rows), keys], 1),
                jnp.concatenate([pick(prefix_value_rows), values], 1),
            ]
        )

    both = lambda x, y: jnp.concatenate([x[:, :, 0], y[:, :, 0]], -1)
    q_rot = turn_call(queries, both(cosine, cosine), both(-sine, sine))

    place = {c: i for i, c in enumerate(ring)}
    table = jnp.array(
        [[ring[(place[c] - s) % n] for s in range(n)] for c in range(n)], jnp.int32
    )
    sources = lax.dynamic_slice(table, (ctx, 0), (1, n)).reshape(n)
    live = jnp.where(partial == 0, cached_len[0], cached_len[1])
    scalars = jnp.concatenate([partial[None], live[None], new_len, sources, block_order])

    forward = [(ring[i], ring[(i + 1) % n]) for i in range(n)]
    backward = [(b, a) for a, b in forward]

    def send(x, way):
        return lax.ppermute(x, "ctx", way)

    firsts = list(range(0, kv_heads, unit))
    count_u = len(firsts)
    own = [payload(slice(h, h + unit)) for h in firsts]
    ahead, back, carry = list(own), list(own), [None] * count_u
    out = None

    parts = [{0: own[u]} for u in range(count_u)]
    local = prefix_key_rows.shape[1]
    steps = plan(n, local // count)

    def step(u, s, last=False):
        return step_call(
            scalars,
            q_rot,
            carry[u],
            parts[u],
            steps[s - 1],
            out,
            last,
            firsts[u],
            blocks,
            n,
            group,
        )

    for u in range(count_u):
        ahead[u], back[u] = send(ahead[u], forward), send(back[u], backward)
    for s in range(1, n // 2):
        for u in range(count_u):
            here, there = ahead[u], back[u]
            parts[u][s], parts[u][n - s] = here, there
            if s + 1 == n // 2:
                here, there = here[0], there[1]
            ahead[u], back[u] = send(here, forward), send(there, backward)
            carry[u] = step(u, s)
    for u in range(count_u):
        parts[u][n // 2] = (ahead[u], back[u])
        out = step(u, n // 2, last=True)
    return out


def solution(mesh):
    ring = ring_order(mesh)
    return jax.shard_map(
        functools.partial(shards, ring),
        mesh=mesh,
        in_specs=(
            P("batch", "ctx", "tp", None),
            P("batch", "ctx", "tp", None),
            P("batch", "ctx", "tp", None),
            P("batch", "ctx", "tp", None),
            P("batch", "ctx", "tp", None),
            P("batch"),
            P("batch"),
            P("batch"),
            P(),
        ),
        out_specs=P("batch", "ctx", "tp", None),
        check_vma=False,
    )
```

```python
import functools

import jax
import jax.numpy as jnp
from jax import lax
from jax.experimental import pallas as pl
from jax.experimental.pallas import tpu as pltpu
from jax.sharding import PartitionSpec as P


rope_base = 500000.0
neg_large = -1e30
log2e = 1.4426950408889634
streams = 2
chunk_units = 2
far = 1 << 29


def ring_order(mesh):
    n = mesh.shape["ctx"]
    plain = list(range(n))
    choices = [
        plain[0::2] + plain[1::2][::-1],
        plain[: n // 2] + plain[n // 2 :][::-1],
        plain,
    ]
    axis = mesh.axis_names.index("ctx")
    line = mesh.devices
    for k in reversed(range(line.ndim)):
        if k != axis:
            line = line.take(0, axis=k)

    def length(order):
        total = 0
        for a, b in zip(order, order[1:] + order[:1]):
            ca, cb = (getattr(line[i], "coords", (i,)) for i in (a, b))
            total += sum(abs(u - v) for u, v in zip(ca, cb))
        return total

    return min(choices, key=length)


def rotate(x, cosine, sine):
    half = x.shape[-1] // 2
    wide = x.astype(jnp.float32)
    first = wide[..., :half]
    second = wide[..., half:]
    return jnp.concatenate(
        [first * cosine - second * sine, second * cosine + first * sine], -1
    ).astype(jnp.bfloat16)


def over_sublanes(op, x):
    for shift in (4, 2, 1):
        x = op(x, pltpu.roll(x, shift, 0))
    return x


def largest(s, top_ref):
    top_ref[...] = over_sublanes(jnp.maximum, jnp.max(s.reshape(-1, 8, s.shape[1]), axis=0))


def scores(q, k, s_ref, top_ref):
    s = lax.dot_general(k, q, (((1,), (1,)), ((), ())), preferred_element_type=jnp.float32)
    s_ref[...] = s
    largest(s, top_ref)


def absorb(tile, vt, s_ref, top_ref, m_ref, l_ref, acc_ref):
    size, width = acc_ref.shape[1:]
    factor = log2e / size**0.5
    before = m_ref[tile]
    top = jnp.maximum(before, top_ref[...])
    alpha = jnp.exp2((before - top) * factor)
    prob = jnp.exp2(s_ref[...].reshape(-1, 8, width) * factor - top * factor)
    l_ref[tile] = l_ref[tile] * alpha + jnp.sum(prob, axis=0)
    m_ref[tile] = top
    prob = prob.reshape(s_ref.shape).astype(jnp.bfloat16)
    acc = (acc_ref[tile].reshape(-1, 8, width) * alpha).reshape(size, width)
    acc_ref[tile] = acc + jnp.dot(vt, prob, preferred_element_type=jnp.float32)


def hide(token, runs, s_ref, top_ref):
    size = s_ref.shape[0] // len(runs)
    tops = []
    for i, (base, offset, limit) in enumerate(runs):
        bound = jnp.minimum(token + offset, limit) - base
        key = lax.broadcasted_iota(jnp.int32, (size, s_ref.shape[1]), 0)
        s = jnp.where(key <= bound, s_ref[i * size : (i + 1) * size], neg_large)
        s_ref[i * size : (i + 1) * size] = s
        tops.append(jnp.max(s.reshape(-1, 8, s.shape[1]), axis=0))
    top_ref[...] = over_sublanes(jnp.maximum, functools.reduce(jnp.maximum, tops))


def plan(n, cache_units):
    half = n // 2
    steps, cache, partial, prefill = [], [], [], []
    for s in range(half + 1):
        for source in [s] if s in (0, half) else [s, n - s]:
            cache += [(source, c) for c in range(cache_units)]
            partial += [(source, None)]
            prefill += [(source, None)]
        chunks = []
        for kind, queue in ((0, cache), (0, partial), (1, prefill)):
            while len(queue) >= chunk_units or (s == half and queue):
                chunks.append((kind, tuple(queue[:chunk_units])))
                del queue[:chunk_units]
        steps.append(chunks)
    return steps


def step_kernel(cfg, sc, q_ref, *refs):
    n, blocks, blk, first_head, chunks, sources, packed, fresh, last, chained = cfg
    refs = list(refs)
    take = lambda k: [refs.pop(0) for _ in range(k)]
    carry = [] if fresh else take(3)
    pairs = {}
    for source, one in zip(sources, packed):
        if one:
            (ref,) = take(1)
            pairs[source] = (ref.at[0], ref.at[1])
        else:
            pairs[source] = tuple(take(2))
    if chained:
        take(1)
    if last:
        (o_ref,) = take(1)
        acc_ref, m_ref, l_ref = refs[-3:]
        stage, o_sem = refs[-5:-3]
    else:
        acc_ref, m_ref, l_ref = take(3)
    kbuf, vt_ref, s0, s1, t0, t1, work = take(7)
    rows, count, _, size = q_ref.shape
    heads = pairs[sources[0]][0].shape[0]
    width = acc_ref.shape[2]
    group = width // blk
    per = blocks // n
    tiles = rows * per
    local = pairs[sources[0]][0].shape[1] - rows * count
    runs = s0.shape[0] // blk
    order = 4 + n
    row_of = lambda kind: sc[0] if kind == 0 else 1 - sc[0]
    run_at = 5

    cached, fresh_runs = [], []
    for i, (kind, units) in enumerate(chunks):
        row = row_of(kind)
        live = sc[2 + row]
        table = []
        for h in range(heads):
            keys, values = [], []
            for source, c in units:
                k_ref, v_ref = pairs[source]
                start = local + row * count if c is None else c * count
                at = pl.ds(start if c is not None else pl.multiple_of(start, count), count)
                keys.append(k_ref[h, at])
                values.append(v_ref[h, at])
            rest = s0.shape[0] - len(units) * count
            if rest:
                keys.append(jnp.zeros((rest, size), keys[0].dtype))
                values.append(jnp.zeros((rest, size), keys[0].dtype))
            kbuf[h * len(chunks) + i] = jnp.concatenate(keys, 0)
            vt_ref[h * len(chunks) + i] = jnp.concatenate(values, 0).T
        hit, cut, new = jnp.int32(0), jnp.int32(int(len(units) < chunk_units)), []
        for source, c in units:
            if c is None:
                for b in range(per):
                    base = sc[order + sc[4 + source] * per + b] * blk
                    table.append((base, 0, live - 1))
                    new.append(base)
            else:
                base = sc[4 + source] * local + c * count
                table += [(base + b * blk, far, sc[1] - 1) for b in range(per)]
                hit = hit | (base < sc[1]).astype(jnp.int32)
                cut = cut | (base + count > sc[1]).astype(jnp.int32)
        cached.append((hit, cut))
        fresh_runs.append(new)
        table += [(0, 0, -1)] * (runs - len(table))
        for run, entry in enumerate(table):
            for j, value in enumerate(entry):
                work[run_at + 3 * run + j, i] = value

    if fresh:
        acc_ref[...] = jnp.zeros_like(acc_ref)
        m_ref[...] = jnp.full_like(m_ref, neg_large)
        l_ref[...] = jnp.zeros_like(l_ref)
    else:
        acc_ref[...] = carry[0][...]
        m_ref[...] = carry[1][...]
        l_ref[...] = carry[2][...]

    total = jnp.int32(0)
    for i, (kind, _) in enumerate(chunks):
        row = row_of(kind)
        for b in range(per):
            first = sc[order + sc[4] * per + b] * blk

            state = list(cached[i])
            least = jnp.minimum(first, sc[2 + row] - 1)
            most = jnp.minimum(first + blk, sc[2 + row]) - 1
            for base in fresh_runs[i]:
                state[0] = state[0] | (base <= most).astype(jnp.int32)
                state[1] = state[1] | (base + blk - 1 > least).astype(jnp.int32)
            go = jnp.where(first < sc[2 + row], state[0], 0)
            for h in range(heads):
                work[0, total] = (h * rows + row) * per + b
                work[1, total] = h * len(chunks) + i
                work[2, total] = state[1]
                work[3, total] = first
                work[4, total] = i
                total = total + go
    none = len(chunks)
    for run in range(runs):
        for j, value in enumerate((0, 0, -1)):
            work[run_at + 3 * run + j, none] = value
    work[0, total] = work[0, jnp.maximum(total - 1, 0)]
    work[0, total + 1] = 0
    for extra in range(2):
        work[1, total + extra] = 0
        work[2, total + extra] = 1
        work[3, total + extra] = 0
        work[4, total + extra] = none

    def prepare(at, s_ref, t_ref):
        tile = work[0, at]
        h, r, b = tile // tiles, (tile // per) % rows, tile % per
        heads_at = pl.ds(pl.multiple_of((first_head + h) * group, group), group)
        q = q_ref[r, pl.ds(b * blk, blk), heads_at, :].reshape(width, size)
        scores(q, kbuf[work[1, at]], s_ref, t_ref)

    def fix(at, s_ref, t_ref):
        @pl.when(work[2, at] == 1)
        def _():
            i = work[4, at]
            token = work[3, at] + lax.broadcasted_iota(jnp.int32, (1, width), 1) // group
            table = [[work[run_at + 3 * run + j, i] for j in range(3)] for run in range(runs)]
            hide(token, table, s_ref, t_ref)

    def finish(at, s_ref, t_ref):
        absorb(work[0, at], vt_ref[work[1, at]], s_ref, t_ref, m_ref, l_ref, acc_ref)

    @pl.when(total > 0)
    def _():
        prepare(0, s0, t0)
        fix(0, s0, t0)

    def body(i, _):
        prepare(2 * i + 1, s1, t1)
        finish(2 * i, s0, t0)
        fix(2 * i + 1, s1, t1)
        prepare(2 * i + 2, s0, t0)
        finish(2 * i + 1, s1, t1)
        fix(2 * i + 2, s0, t0)
        return 0

    lax.fori_loop(0, (total + 1) // 2, body, 0)

    if last:

        def write(tile):
            h, r, b = tile // tiles, (tile // per) % rows, tile % per
            heads_at = pl.ds(pl.multiple_of((first_head + h) * group, group), group)
            return pltpu.make_async_copy(
                stage.at[tile], o_ref.at[r, pl.ds(b * blk, blk), heads_at], o_sem.at[tile]
            )

        def store(tile, _):
            r, b = (tile // per) % rows, tile % per
            first = sc[order + sc[4] * per + b] * blk
            live = sc[2 + r]

            @pl.when(first >= live)
            def _():
                stage[tile] = jnp.zeros(stage.shape[1:], stage.dtype)

            @pl.when(first < live)
            def _():
                sums = over_sublanes(jnp.add, l_ref[tile])
                out = (acc_ref[tile].reshape(-1, 8, width) / sums).reshape(size, width)
                query = lax.broadcasted_iota(jnp.int32, (1, width), 1)
                out = jnp.where(query < (live - first) * group, out, 0.0)
                stage[tile] = out.astype(stage.dtype).T.reshape(stage.shape[1:])

            write(tile).start()
            return 0

        lax.fori_loop(0, heads * tiles, store, 0)
        lax.fori_loop(0, heads * tiles, lambda t, _: (write(t).wait(), 0)[1], 0)


def step_call(scalars, q_rot, carry, parts, chunks, out, last, first_head, blocks, n, group):
    rows, count, _, size = q_rot.shape
    sources = sorted({source for _, units in chunks for source, _ in units})
    packed = tuple(not isinstance(parts[source], tuple) for source in sources)
    arrays = []
    for source in sources:
        arrays += list(parts[source]) if isinstance(parts[source], tuple) else [parts[source]]
    unit_heads = arrays[0].shape[-3]
    per = blocks // n
    blk = count // per
    width = blk * group
    tiles = unit_heads * rows * per
    depth = chunk_units * count
    items = unit_heads * per * len(chunks)
    fresh, chained = carry is None, last and out is not None
    vmem, anywhere = pl.BlockSpec(memory_space=pltpu.VMEM), pl.BlockSpec(memory_space=pl.ANY)
    state = lambda d: (tiles, d, width)
    f32 = lambda d: jax.ShapeDtypeStruct(state(d), jnp.float32)
    scratch = [
        pltpu.VMEM((unit_heads * len(chunks), depth, size), jnp.bfloat16),
        pltpu.VMEM((unit_heads * len(chunks), size, depth), jnp.bfloat16),
        pltpu.VMEM((depth, width), jnp.float32),
        pltpu.VMEM((depth, width), jnp.float32),
        pltpu.VMEM((8, width), jnp.float32),
        pltpu.VMEM((8, width), jnp.float32),
        pltpu.SMEM((5 + 3 * depth // blk, items + 2), jnp.int32),
    ]
    operands = [scalars, q_rot] + ([] if fresh else list(carry)) + arrays
    specs = [pl.BlockSpec(memory_space=pltpu.SMEM)] + [vmem] * (len(operands) - 1)
    aliases = {} if fresh or last else {2: 0, 3: 1, 4: 2}
    if last:
        scratch += [
            pltpu.VMEM((tiles, blk, group, size), jnp.bfloat16),
            pltpu.SemaphoreType.DMA((tiles,)),
        ] + [pltpu.VMEM(state(d), jnp.float32) for d in (size, 8, 8)]
        if chained:
            operands.append(out)
            specs.append(anywhere)
            aliases = {len(operands) - 1: 0}
        shapes, out_specs = jax.ShapeDtypeStruct(q_rot.shape, q_rot.dtype), anywhere
    else:
        shapes, out_specs = [f32(size), f32(8), f32(8)], [vmem] * 3
    cfg = (n, blocks, blk, first_head, chunks, sources, packed, fresh, last, chained)
    pairs = items * depth * width
    return pl.pallas_call(
        functools.partial(step_kernel, cfg),
        in_specs=specs,
        out_specs=out_specs,
        scratch_shapes=scratch,
        out_shape=shapes,
        input_output_aliases=aliases,
        compiler_params=pltpu.CompilerParams(vmem_limit_bytes=24 * 1024 * 1024),
        cost_estimate=pl.CostEstimate(
            flops=pairs * size * 4, bytes_accessed=1024 * 1024, transcendentals=pairs
        ),
    )(*operands)


def turn_kernel(parts, q_ref, cosine_ref, sine_ref, o_ref):
    i = pl.program_id(0)
    tokens, _, size = q_ref.shape[1:]
    x = q_ref[0].astype(jnp.float32)
    cosine = cosine_ref[0][:, None, :]
    sine = sine_ref[0][:, None, :]
    turned = x * cosine + pltpu.roll(x, size // 2, 2) * sine
    at = pl.ds(pl.multiple_of((i % parts) * tokens, tokens), tokens)
    o_ref[i // parts, at] = turned.astype(o_ref.dtype)


def turn_call(queries, cosine, sine):
    rows, count, heads, size = queries.shape
    tokens = count // 2
    parts = count // tokens
    table = pl.BlockSpec((1, tokens, size), lambda i: (i // parts, i % parts, 0))
    return pl.pallas_call(
        functools.partial(turn_kernel, parts),
        grid=(rows * parts,),
        in_specs=[
            pl.BlockSpec((1, tokens, heads, size), lambda i: (i // parts, i % parts, 0, 0)),
            table,
            table,
        ],
        out_specs=pl.BlockSpec(queries.shape, lambda i: (0, 0, 0, 0)),
        out_shape=jax.ShapeDtypeStruct(queries.shape, queries.dtype),
        compiler_params=pltpu.CompilerParams(vmem_limit_bytes=10 * 1024 * 1024),
        cost_estimate=pl.CostEstimate(
            flops=queries.size * 4, bytes_accessed=queries.size * 4, transcendentals=0
        ),
        name="turn",
    )(pltpu.with_memory_space_constraint(queries, pltpu.HBM), cosine, sine)


def shards(
    ring,
    queries,
    span_key_rows,
    span_value_rows,
    prefix_key_rows,
    prefix_value_rows,
    cached_len,
    new_len,
    prefill_flag,
    block_order,
):
    n = len(ring)
    rows, count, heads, size = queries.shape
    kv_heads = span_key_rows.shape[2]
    group = heads // kv_heads
    blocks = block_order.shape[0]
    per = blocks // n
    blk = count // per
    ctx = lax.axis_index("ctx")

    partial = jnp.where(prefill_flag[0] == 0, 0, 1).astype(jnp.int32)
    half = size // 2
    mine = lax.dynamic_slice(block_order, (ctx * per,), (per,))
    q_index = (mine[:, None] * blk + jnp.arange(blk, dtype=jnp.int32)[None, :]).reshape(count)
    base = jnp.where(prefill_flag == 1, 0, cached_len)
    positions = base[:, None] + q_index[None, :]
    inverse = rope_base ** (-(jnp.arange(half, dtype=jnp.float32) * 2.0 / size))
    angle = positions.astype(jnp.float32)[:, :, None, None] * inverse
    cosine = jnp.cos(angle)
    sine = jnp.sin(angle)
    unit = -(-kv_heads // streams)

    def payload(at):
        pick = lambda x: jnp.swapaxes(jnp.where(partial == 0, x[0], x[1])[:, at], 0, 1)
        new = lambda x: jnp.moveaxis(x, 2, 0).reshape(x.shape[2], rows * count, size)
        keys = new(rotate(span_key_rows[:, :, at], cosine, sine))
        values = new(span_value_rows[:, :, at])
        return jnp.stack(
            [
                jnp.concatenate([pick(prefix_key_rows), keys], 1),
                jnp.concatenate([pick(prefix_value_rows), values], 1),
            ]
        )

    both = lambda x, y: jnp.concatenate([x[:, :, 0], y[:, :, 0]], -1)
    q_rot = turn_call(queries, both(cosine, cosine), both(-sine, sine))

    place = {c: i for i, c in enumerate(ring)}
    table = jnp.array(
        [[ring[(place[c] - s) % n] for s in range(n)] for c in range(n)], jnp.int32
    )
    sources = lax.dynamic_slice(table, (ctx, 0), (1, n)).reshape(n)
    live = jnp.where(partial == 0, cached_len[0], cached_len[1])
    scalars = jnp.concatenate([partial[None], live[None], new_len, sources, block_order])

    forward = [(ring[i], ring[(i + 1) % n]) for i in range(n)]
    backward = [(b, a) for a, b in forward]

    def send(x, way):
        return lax.ppermute(x, "ctx", way)

    firsts = list(range(0, kv_heads, unit))
    count_u = len(firsts)
    own = [payload(slice(h, h + unit)) for h in firsts]
    ahead, back, carry = list(own), list(own), [None] * count_u
    out = None

    parts = [{0: own[u]} for u in range(count_u)]
    local = prefix_key_rows.shape[1]
    steps = plan(n, local // count)

    def step(u, s, last=False):
        return step_call(
            scalars,
            q_rot,
            carry[u],
            parts[u],
            steps[s],
            out,
            last,
            firsts[u],
            blocks,
            n,
            group,
        )

    for u in range(count_u):
        ahead[u], back[u] = send(ahead[u], forward), send(back[u], backward)
    for u in range(count_u):
        carry[u] = step(u, 0)
    for s in range(1, n // 2):
        for u in range(count_u):
            here, there = ahead[u], back[u]
            parts[u][s], parts[u][n - s] = here, there
            if s + 1 == n // 2:
                here, there = here[0], there[1]
            ahead[u], back[u] = send(here, forward), send(there, backward)
            carry[u] = step(u, s)
    for u in range(count_u):
        parts[u][n // 2] = (ahead[u], back[u])
        out = step(u, n // 2, last=True)
    return out


def solution(mesh):
    ring = ring_order(mesh)
    return jax.shard_map(
        functools.partial(shards, ring),
        mesh=mesh,
        in_specs=(
            P("batch", "ctx", "tp", None),
            P("batch", "ctx", "tp", None),
            P("batch", "ctx", "tp", None),
            P("batch", "ctx", "tp", None),
            P("batch", "ctx", "tp", None),
            P("batch"),
            P("batch"),
            P("batch"),
            P(),
        ),
        out_specs=P("batch", "ctx", "tp", None),
        check_vma=False,
    )
```

```python
import functools

import jax
import jax.numpy as jnp
from jax import lax
from jax.experimental import pallas as pl
from jax.experimental.pallas import tpu as pltpu
from jax.sharding import PartitionSpec as P


rope_base = 500000.0
neg_large = -1e30
log2e = 1.4426950408889634
streams = 2
chunk_units = 2
lane_step = 256
far = 1 << 29


def ring_order(mesh):
    n = mesh.shape["ctx"]
    plain = list(range(n))
    choices = [
        plain[0::2] + plain[1::2][::-1],
        plain[: n // 2] + plain[n // 2 :][::-1],
        plain,
    ]
    axis = mesh.axis_names.index("ctx")
    line = mesh.devices
    for k in reversed(range(line.ndim)):
        if k != axis:
            line = line.take(0, axis=k)

    def length(order):
        total = 0
        for a, b in zip(order, order[1:] + order[:1]):
            ca, cb = (getattr(line[i], "coords", (i,)) for i in (a, b))
            total += sum(abs(u - v) for u, v in zip(ca, cb))
        return total

    return min(choices, key=length)


def rotate(x, cosine, sine):
    half = x.shape[-1] // 2
    wide = x.astype(jnp.float32)
    first = wide[..., :half]
    second = wide[..., half:]
    return jnp.concatenate(
        [first * cosine - second * sine, second * cosine + first * sine], -1
    ).astype(jnp.bfloat16)


def over_sublanes(op, x):
    for shift in (4, 2, 1):
        x = op(x, pltpu.roll(x, shift, 0))
    return x


def largest(s):
    return over_sublanes(jnp.maximum, jnp.max(s.reshape(-1, 8, s.shape[1]), axis=0))


def scores(q, k, s_ref, top_ref, at):
    s = lax.dot_general(k, q, (((1,), (1,)), ((), ())), preferred_element_type=jnp.float32)
    s_ref[:, at] = s
    top_ref[:, at] = largest(s)


def absorb(tile, vt, s_ref, top_ref, m_ref, l_ref, acc_ref, at):
    s = s_ref[:, at]
    size, width = vt.shape[0], s.shape[1]
    factor = log2e / size**0.5
    before = m_ref[tile, :, at]
    top = jnp.maximum(before, top_ref[:, at])
    alpha = jnp.exp2((before - top) * factor)
    prob = jnp.exp2(s.reshape(-1, 8, width) * factor - top * factor)
    l_ref[tile, :, at] = l_ref[tile, :, at] * alpha + jnp.sum(prob, axis=0)
    m_ref[tile, :, at] = top
    prob = prob.reshape(s.shape).astype(jnp.bfloat16)
    acc = (acc_ref[tile, :, at].reshape(-1, 8, width) * alpha).reshape(size, width)
    acc_ref[tile, :, at] = acc + jnp.dot(vt, prob, preferred_element_type=jnp.float32)


def hide(token, runs, s_ref, top_ref):
    size = s_ref.shape[0] // len(runs)
    tops = []
    for i, (base, offset, limit) in enumerate(runs):
        bound = jnp.minimum(token + offset, limit) - base
        key = lax.broadcasted_iota(jnp.int32, (size, s_ref.shape[1]), 0)
        s = jnp.where(key <= bound, s_ref[i * size : (i + 1) * size], neg_large)
        s_ref[i * size : (i + 1) * size] = s
        tops.append(jnp.max(s.reshape(-1, 8, s.shape[1]), axis=0))
    top_ref[...] = over_sublanes(jnp.maximum, functools.reduce(jnp.maximum, tops))


def plan(n, cache_units):
    half = n // 2
    steps, cache, partial, prefill = [], [], [], []
    for s in range(half + 1):
        for source in [s] if s in (0, half) else [s, n - s]:
            cache += [(source, c) for c in range(cache_units)]
            partial += [(source, None)]
            prefill += [(source, None)]
        chunks = []
        for kind, queue in ((0, cache), (0, partial), (1, prefill)):
            while len(queue) >= chunk_units or (s == half and queue):
                chunks.append((kind, tuple(queue[:chunk_units])))
                del queue[:chunk_units]
        steps.append(chunks)
    return steps


def step_kernel(cfg, sc, q_ref, *refs):
    n, blocks, blk, first_head, chunks, sources, packed, fresh, last, chained = cfg
    refs = list(refs)
    take = lambda k: [refs.pop(0) for _ in range(k)]
    carry = [] if fresh else take(3)
    pairs = {}
    for source, one in zip(sources, packed):
        if one:
            (ref,) = take(1)
            pairs[source] = (ref.at[0], ref.at[1])
        else:
            pairs[source] = tuple(take(2))
    if chained:
        take(1)
    if last:
        (o_ref,) = take(1)
        acc_ref, m_ref, l_ref = refs[-3:]
        stage, o_sem = refs[-5:-3]
    else:
        acc_ref, m_ref, l_ref = take(3)
    kbuf, vt_ref, s0, s1, t0, t1, work = take(7)
    rows, count, _, size = q_ref.shape
    heads = pairs[sources[0]][0].shape[0]
    width = acc_ref.shape[2]
    group = width // blk
    per = blocks // n
    tiles = rows * per
    local = pairs[sources[0]][0].shape[1] - rows * count
    runs = s0.shape[0] // blk
    order = 4 + n
    row_of = lambda kind: sc[0] if kind == 0 else 1 - sc[0]
    run_at = 5

    cached, fresh_runs = [], []
    for i, (kind, units) in enumerate(chunks):
        row = row_of(kind)
        live = sc[2 + row]
        table = []
        for h in range(heads):
            keys, values = [], []
            for source, c in units:
                k_ref, v_ref = pairs[source]
                start = local + row * count if c is None else c * count
                at = pl.ds(start if c is not None else pl.multiple_of(start, count), count)
                keys.append(k_ref[h, at])
                values.append(v_ref[h, at])
            rest = s0.shape[0] - len(units) * count
            if rest:
                keys.append(jnp.zeros((rest, size), keys[0].dtype))
                values.append(jnp.zeros((rest, size), keys[0].dtype))
            kbuf[h * len(chunks) + i] = jnp.concatenate(keys, 0)
            vt_ref[h * len(chunks) + i] = jnp.concatenate(values, 0).T
        hit, cut, new = jnp.int32(0), jnp.int32(int(len(units) < chunk_units)), []
        for source, c in units:
            if c is None:
                for b in range(per):
                    base = sc[order + sc[4 + source] * per + b] * blk
                    table.append((base, 0, live - 1))
                    new.append(base)
            else:
                base = sc[4 + source] * local + c * count
                table += [(base + b * blk, far, sc[1] - 1) for b in range(per)]
                hit = hit | (base < sc[1]).astype(jnp.int32)
                cut = cut | (base + count > sc[1]).astype(jnp.int32)
        cached.append((hit, cut))
        fresh_runs.append(new)
        table += [(0, 0, -1)] * (runs - len(table))
        for run, entry in enumerate(table):
            for j, value in enumerate(entry):
                work[run_at + 3 * run + j, i] = value

    if fresh:
        acc_ref[...] = jnp.zeros_like(acc_ref)
        m_ref[...] = jnp.full_like(m_ref, neg_large)
        l_ref[...] = jnp.zeros_like(l_ref)
    else:
        acc_ref[...] = carry[0][...]
        m_ref[...] = carry[1][...]
        l_ref[...] = carry[2][...]

    total = jnp.int32(0)
    for i, (kind, _) in enumerate(chunks):
        row = row_of(kind)
        for b in range(per):
            first = sc[order + sc[4] * per + b] * blk

            state = list(cached[i])
            least = jnp.minimum(first, sc[2 + row] - 1)
            most = jnp.minimum(first + blk, sc[2 + row]) - 1
            for base in fresh_runs[i]:
                state[0] = state[0] | (base <= most).astype(jnp.int32)
                state[1] = state[1] | (base + blk - 1 > least).astype(jnp.int32)
            go = jnp.where(first < sc[2 + row], state[0], 0)
            for h in range(heads):
                work[0, total] = (h * rows + row) * per + b
                work[1, total] = h * len(chunks) + i
                work[2, total] = state[1]
                work[3, total] = first
                work[4, total] = i
                total = total + go
    none = len(chunks)
    for run in range(runs):
        for j, value in enumerate((0, 0, -1)):
            work[run_at + 3 * run + j, none] = value
    work[0, total] = work[0, jnp.maximum(total - 1, 0)]
    work[0, total + 1] = 0
    for extra in range(2):
        work[1, total + extra] = 0
        work[2, total + extra] = 1
        work[3, total + extra] = 0
        work[4, total + extra] = none

    lanes = min(lane_step, width)

    def prepare(at, s_ref, t_ref, start):
        tile = work[0, at]
        h, r, b = tile // tiles, (tile // per) % rows, tile % per
        heads_at = pl.ds(pl.multiple_of((first_head + h) * group, group), group)
        tokens_at = pl.ds(b * blk + start // group, lanes // group)
        q = q_ref[r, tokens_at, heads_at, :].reshape(lanes, size)
        scores(q, kbuf[work[1, at]], s_ref, t_ref, slice(start, start + lanes))

    def fix(at, s_ref, t_ref):
        @pl.when(work[2, at] == 1)
        def _():
            i = work[4, at]
            token = work[3, at] + lax.broadcasted_iota(jnp.int32, (1, width), 1) // group
            table = [[work[run_at + 3 * run + j, i] for j in range(3)] for run in range(runs)]
            hide(token, table, s_ref, t_ref)

    def finish(at, s_ref, t_ref, start):
        spot = slice(start, start + lanes)
        absorb(work[0, at], vt_ref[work[1, at]], s_ref, t_ref, m_ref, l_ref, acc_ref, spot)

    @pl.when(total > 0)
    def _():
        for start in range(0, width, lanes):
            prepare(0, s0, t0, start)
        fix(0, s0, t0)

    def body(i, _):
        for start in range(0, width, lanes):
            prepare(2 * i + 1, s1, t1, start)
            finish(2 * i, s0, t0, start)
        fix(2 * i + 1, s1, t1)
        for start in range(0, width, lanes):
            prepare(2 * i + 2, s0, t0, start)
            finish(2 * i + 1, s1, t1, start)
        fix(2 * i + 2, s0, t0)
        return 0

    lax.fori_loop(0, (total + 1) // 2, body, 0)

    if last:

        def write(tile):
            h, r, b = tile // tiles, (tile // per) % rows, tile % per
            heads_at = pl.ds(pl.multiple_of((first_head + h) * group, group), group)
            return pltpu.make_async_copy(
                stage.at[tile], o_ref.at[r, pl.ds(b * blk, blk), heads_at], o_sem.at[tile]
            )

        def store(tile, _):
            r, b = (tile // per) % rows, tile % per
            first = sc[order + sc[4] * per + b] * blk
            live = sc[2 + r]

            @pl.when(first >= live)
            def _():
                stage[tile] = jnp.zeros(stage.shape[1:], stage.dtype)

            @pl.when(first < live)
            def _():
                sums = over_sublanes(jnp.add, l_ref[tile])
                out = (acc_ref[tile].reshape(-1, 8, width) / sums).reshape(size, width)
                query = lax.broadcasted_iota(jnp.int32, (1, width), 1)
                out = jnp.where(query < (live - first) * group, out, 0.0)
                stage[tile] = out.astype(stage.dtype).T.reshape(stage.shape[1:])

            write(tile).start()
            return 0

        lax.fori_loop(0, heads * tiles, store, 0)
        lax.fori_loop(0, heads * tiles, lambda t, _: (write(t).wait(), 0)[1], 0)


def step_call(scalars, q_rot, carry, parts, chunks, out, last, first_head, blocks, n, group):
    rows, count, _, size = q_rot.shape
    sources = sorted({source for _, units in chunks for source, _ in units})
    packed = tuple(not isinstance(parts[source], tuple) for source in sources)
    arrays = []
    for source in sources:
        arrays += list(parts[source]) if isinstance(parts[source], tuple) else [parts[source]]
    unit_heads = arrays[0].shape[-3]
    per = blocks // n
    blk = count // per
    width = blk * group
    tiles = unit_heads * rows * per
    depth = chunk_units * count
    items = unit_heads * per * len(chunks)
    fresh, chained = carry is None, last and out is not None
    vmem, anywhere = pl.BlockSpec(memory_space=pltpu.VMEM), pl.BlockSpec(memory_space=pl.ANY)
    state = lambda d: (tiles, d, width)
    f32 = lambda d: jax.ShapeDtypeStruct(state(d), jnp.float32)
    scratch = [
        pltpu.VMEM((unit_heads * len(chunks), depth, size), jnp.bfloat16),
        pltpu.VMEM((unit_heads * len(chunks), size, depth), jnp.bfloat16),
        pltpu.VMEM((depth, width), jnp.float32),
        pltpu.VMEM((depth, width), jnp.float32),
        pltpu.VMEM((8, width), jnp.float32),
        pltpu.VMEM((8, width), jnp.float32),
        pltpu.SMEM((5 + 3 * depth // blk, items + 2), jnp.int32),
    ]
    operands = [scalars, q_rot] + ([] if fresh else list(carry)) + arrays
    specs = [pl.BlockSpec(memory_space=pltpu.SMEM)] + [vmem] * (len(operands) - 1)
    aliases = {} if fresh or last else {2: 0, 3: 1, 4: 2}
    if last:
        scratch += [
            pltpu.VMEM((tiles, blk, group, size), jnp.bfloat16),
            pltpu.SemaphoreType.DMA((tiles,)),
        ] + [pltpu.VMEM(state(d), jnp.float32) for d in (size, 8, 8)]
        if chained:
            operands.append(out)
            specs.append(anywhere)
            aliases = {len(operands) - 1: 0}
        shapes, out_specs = jax.ShapeDtypeStruct(q_rot.shape, q_rot.dtype), anywhere
    else:
        shapes, out_specs = [f32(size), f32(8), f32(8)], [vmem] * 3
    cfg = (n, blocks, blk, first_head, chunks, sources, packed, fresh, last, chained)
    pairs = items * depth * width
    return pl.pallas_call(
        functools.partial(step_kernel, cfg),
        in_specs=specs,
        out_specs=out_specs,
        scratch_shapes=scratch,
        out_shape=shapes,
        input_output_aliases=aliases,
        compiler_params=pltpu.CompilerParams(vmem_limit_bytes=24 * 1024 * 1024),
        cost_estimate=pl.CostEstimate(
            flops=pairs * size * 4, bytes_accessed=1024 * 1024, transcendentals=pairs
        ),
    )(*operands)


def turn_kernel(parts, q_ref, cosine_ref, sine_ref, o_ref):
    i = pl.program_id(0)
    tokens, _, size = q_ref.shape[1:]
    x = q_ref[0].astype(jnp.float32)
    cosine = cosine_ref[0][:, None, :]
    sine = sine_ref[0][:, None, :]
    turned = x * cosine + pltpu.roll(x, size // 2, 2) * sine
    at = pl.ds(pl.multiple_of((i % parts) * tokens, tokens), tokens)
    o_ref[i // parts, at] = turned.astype(o_ref.dtype)


def turn_call(queries, cosine, sine):
    rows, count, heads, size = queries.shape
    tokens = count // 2
    parts = count // tokens
    table = pl.BlockSpec((1, tokens, size), lambda i: (i // parts, i % parts, 0))
    return pl.pallas_call(
        functools.partial(turn_kernel, parts),
        grid=(rows * parts,),
        in_specs=[
            pl.BlockSpec((1, tokens, heads, size), lambda i: (i // parts, i % parts, 0, 0)),
            table,
            table,
        ],
        out_specs=pl.BlockSpec(queries.shape, lambda i: (0, 0, 0, 0)),
        out_shape=jax.ShapeDtypeStruct(queries.shape, queries.dtype),
        compiler_params=pltpu.CompilerParams(vmem_limit_bytes=10 * 1024 * 1024),
        cost_estimate=pl.CostEstimate(
            flops=queries.size * 4, bytes_accessed=queries.size * 4, transcendentals=0
        ),
        name="turn",
    )(pltpu.with_memory_space_constraint(queries, pltpu.HBM), cosine, sine)


def shards(
    ring,
    queries,
    span_key_rows,
    span_value_rows,
    prefix_key_rows,
    prefix_value_rows,
    cached_len,
    new_len,
    prefill_flag,
    block_order,
):
    n = len(ring)
    rows, count, heads, size = queries.shape
    kv_heads = span_key_rows.shape[2]
    group = heads // kv_heads
    blocks = block_order.shape[0]
    per = blocks // n
    blk = count // per
    ctx = lax.axis_index("ctx")

    partial = jnp.where(prefill_flag[0] == 0, 0, 1).astype(jnp.int32)
    half = size // 2
    mine = lax.dynamic_slice(block_order, (ctx * per,), (per,))
    q_index = (mine[:, None] * blk + jnp.arange(blk, dtype=jnp.int32)[None, :]).reshape(count)
    base = jnp.where(prefill_flag == 1, 0, cached_len)
    positions = base[:, None] + q_index[None, :]
    inverse = rope_base ** (-(jnp.arange(half, dtype=jnp.float32) * 2.0 / size))
    angle = positions.astype(jnp.float32)[:, :, None, None] * inverse
    cosine = jnp.cos(angle)
    sine = jnp.sin(angle)
    unit = -(-kv_heads // streams)

    def payload(at):
        pick = lambda x: jnp.swapaxes(jnp.where(partial == 0, x[0], x[1])[:, at], 0, 1)
        new = lambda x: jnp.moveaxis(x, 2, 0).reshape(x.shape[2], rows * count, size)
        keys = new(rotate(span_key_rows[:, :, at], cosine, sine))
        values = new(span_value_rows[:, :, at])
        return jnp.stack(
            [
                jnp.concatenate([pick(prefix_key_rows), keys], 1),
                jnp.concatenate([pick(prefix_value_rows), values], 1),
            ]
        )

    both = lambda x, y: jnp.concatenate([x[:, :, 0], y[:, :, 0]], -1)
    q_rot = turn_call(queries, both(cosine, cosine), both(-sine, sine))

    place = {c: i for i, c in enumerate(ring)}
    table = jnp.array(
        [[ring[(place[c] - s) % n] for s in range(n)] for c in range(n)], jnp.int32
    )
    sources = lax.dynamic_slice(table, (ctx, 0), (1, n)).reshape(n)
    live = jnp.where(partial == 0, cached_len[0], cached_len[1])
    scalars = jnp.concatenate([partial[None], live[None], new_len, sources, block_order])

    forward = [(ring[i], ring[(i + 1) % n]) for i in range(n)]
    backward = [(b, a) for a, b in forward]

    def send(x, way):
        return lax.ppermute(x, "ctx", way)

    firsts = list(range(0, kv_heads, unit))
    count_u = len(firsts)
    own = [payload(slice(h, h + unit)) for h in firsts]
    ahead, back, carry = list(own), list(own), [None] * count_u
    out = None

    parts = [{0: own[u]} for u in range(count_u)]
    local = prefix_key_rows.shape[1]
    steps = plan(n, local // count)

    def step(u, s, last=False):
        return step_call(
            scalars,
            q_rot,
            carry[u],
            parts[u],
            steps[s],
            out,
            last,
            firsts[u],
            blocks,
            n,
            group,
        )

    for u in range(count_u):
        ahead[u], back[u] = send(ahead[u], forward), send(back[u], backward)
    for u in range(count_u):
        carry[u] = step(u, 0)
    for s in range(1, n // 2):
        for u in range(count_u):
            here, there = ahead[u], back[u]
            parts[u][s], parts[u][n - s] = here, there
            if s + 1 == n // 2:
                here, there = here[0], there[1]
            ahead[u], back[u] = send(here, forward), send(there, backward)
            carry[u] = step(u, s)
    for u in range(count_u):
        parts[u][n // 2] = (ahead[u], back[u])
        out = step(u, n // 2, last=True)
    return out


def solution(mesh):
    ring = ring_order(mesh)
    return jax.shard_map(
        functools.partial(shards, ring),
        mesh=mesh,
        in_specs=(
            P("batch", "ctx", "tp", None),
            P("batch", "ctx", "tp", None),
            P("batch", "ctx", "tp", None),
            P("batch", "ctx", "tp", None),
            P("batch", "ctx", "tp", None),
            P("batch"),
            P("batch"),
            P("batch"),
            P(),
        ),
        out_specs=P("batch", "ctx", "tp", None),
        check_vma=False,
    )
```

```python
import functools

import jax
import jax.numpy as jnp
from jax import lax
from jax.experimental import pallas as pl
from jax.experimental.pallas import tpu as pltpu
from jax.sharding import PartitionSpec as P


rope_base = 500000.0
neg_large = -1e30
log2e = 1.4426950408889634
streams = 2
chunk_units = 2
lane_step = 256
far = 1 << 29


def ring_order(mesh):
    n = mesh.shape["ctx"]
    plain = list(range(n))
    choices = [
        plain[0::2] + plain[1::2][::-1],
        plain[: n // 2] + plain[n // 2 :][::-1],
        plain,
    ]
    axis = mesh.axis_names.index("ctx")
    line = mesh.devices
    for k in reversed(range(line.ndim)):
        if k != axis:
            line = line.take(0, axis=k)

    def length(order):
        total = 0
        for a, b in zip(order, order[1:] + order[:1]):
            ca, cb = (getattr(line[i], "coords", (i,)) for i in (a, b))
            total += sum(abs(u - v) for u, v in zip(ca, cb))
        return total

    return min(choices, key=length)


def rotate(x, cosine, sine):
    half = x.shape[-1] // 2
    wide = x.astype(jnp.float32)
    first = wide[..., :half]
    second = wide[..., half:]
    return jnp.concatenate(
        [first * cosine - second * sine, second * cosine + first * sine], -1
    ).astype(jnp.bfloat16)


def over_sublanes(op, x):
    for shift in (4, 2, 1):
        x = op(x, pltpu.roll(x, shift, 0))
    return x


def largest(s):
    return over_sublanes(jnp.maximum, jnp.max(s.reshape(-1, 8, s.shape[1]), axis=0))


def scores(q, k, s_ref, top_ref, at):
    s = lax.dot_general(k, q, (((1,), (1,)), ((), ())), preferred_element_type=jnp.float32)
    s_ref[:, at] = s
    top_ref[:, at] = largest(s)


def absorb(tile, vt, s_ref, top_ref, m_ref, l_ref, acc_ref, at):
    s = s_ref[:, at]
    size, width = vt.shape[0], s.shape[1]
    factor = log2e / size**0.5
    before = m_ref[tile, :, at]
    top = jnp.maximum(before, top_ref[:, at])
    alpha = jnp.exp2((before - top) * factor)
    prob = jnp.exp2(s.reshape(-1, 8, width) * factor - top * factor)
    l_ref[tile, :, at] = l_ref[tile, :, at] * alpha + jnp.sum(prob, axis=0)
    m_ref[tile, :, at] = top
    prob = prob.reshape(s.shape).astype(jnp.bfloat16)
    acc = (acc_ref[tile, :, at].reshape(-1, 8, width) * alpha).reshape(size, width)
    acc_ref[tile, :, at] = acc + jnp.dot(vt, prob, preferred_element_type=jnp.float32)


def hide(token, run, count, s_ref, top_ref):
    size, width = s_ref.shape[0] // count, s_ref.shape[1]

    def one(i, top):
        base, offset, limit = run(i)
        at = pl.ds(pl.multiple_of(i * size, size), size)
        key = lax.broadcasted_iota(jnp.int32, (size, width), 0)
        s = jnp.where(key <= jnp.minimum(token + offset, limit) - base, s_ref[at, :], neg_large)
        s_ref[at, :] = s
        return jnp.maximum(top, jnp.max(s.reshape(-1, 8, width), axis=0))

    top = lax.fori_loop(0, count, one, jnp.full((8, width), neg_large, jnp.float32))
    top_ref[...] = over_sublanes(jnp.maximum, top)


def plan(n, cache_units):
    half = n // 2
    steps, cache, partial, prefill = [], [], [], []
    for s in range(half + 1):
        for source in [s] if s in (0, half) else [s, n - s]:
            cache += [(source, c) for c in range(cache_units)]
            partial += [(source, None)]
            prefill += [(source, None)]
        chunks = []
        for kind, queue in ((0, cache), (0, partial), (1, prefill)):
            while len(queue) >= chunk_units or (s == half and queue):
                chunks.append((kind, tuple(queue[:chunk_units])))
                del queue[:chunk_units]
        steps.append(chunks)
    return steps


def step_kernel(cfg, sc, q_ref, *refs):
    n, blocks, blk, first_head, chunks, sources, packed, fresh, last, chained = cfg
    refs = list(refs)
    take = lambda k: [refs.pop(0) for _ in range(k)]
    carry = [] if fresh else take(3)
    pairs = {}
    for source, one in zip(sources, packed):
        if one:
            (ref,) = take(1)
            pairs[source] = (ref.at[0], ref.at[1])
        else:
            pairs[source] = tuple(take(2))
    if chained:
        take(1)
    if last:
        (o_ref,) = take(1)
        acc_ref, m_ref, l_ref = refs[-3:]
        stage, o_sem = refs[-5:-3]
    else:
        acc_ref, m_ref, l_ref = take(3)
    kbuf, vt_ref, s0, s1, s2, s3, t0, t1, t2, t3, work = take(11)
    rows, count, _, size = q_ref.shape
    heads = pairs[sources[0]][0].shape[0]
    width = acc_ref.shape[2]
    group = width // blk
    per = blocks // n
    tiles = rows * per
    local = pairs[sources[0]][0].shape[1] - rows * count
    runs = s0.shape[0] // blk
    order = 4 + n
    row_of = lambda kind: sc[0] if kind == 0 else 1 - sc[0]
    run_at = 5

    cached, fresh_runs = [], []
    for i, (kind, units) in enumerate(chunks):
        row = row_of(kind)
        live = sc[2 + row]
        table = []
        for h in range(heads):
            keys, values = [], []
            for source, c in units:
                k_ref, v_ref = pairs[source]
                start = local + row * count if c is None else c * count
                at = pl.ds(start if c is not None else pl.multiple_of(start, count), count)
                keys.append(k_ref[h, at])
                values.append(v_ref[h, at])
            rest = s0.shape[0] - len(units) * count
            if rest:
                keys.append(jnp.zeros((rest, size), keys[0].dtype))
                values.append(jnp.zeros((rest, size), keys[0].dtype))
            kbuf[h * len(chunks) + i] = jnp.concatenate(keys, 0)
            vt_ref[h * len(chunks) + i] = jnp.concatenate(values, 0).T
        hit, cut, new = jnp.int32(0), jnp.int32(int(len(units) < chunk_units)), []
        for source, c in units:
            if c is None:
                for b in range(per):
                    base = sc[order + sc[4 + source] * per + b] * blk
                    table.append((base, 0, live - 1))
                    new.append(base)
            else:
                base = sc[4 + source] * local + c * count
                table += [(base + b * blk, far, sc[1] - 1) for b in range(per)]
                hit = hit | (base < sc[1]).astype(jnp.int32)
                cut = cut | (base + count > sc[1]).astype(jnp.int32)
        cached.append((hit, cut))
        fresh_runs.append(new)
        table += [(0, 0, -1)] * (runs - len(table))
        for run, entry in enumerate(table):
            for j, value in enumerate(entry):
                work[run_at + 3 * run + j, i] = value

    if fresh:
        acc_ref[...] = jnp.zeros_like(acc_ref)
        m_ref[...] = jnp.full_like(m_ref, neg_large)
        l_ref[...] = jnp.zeros_like(l_ref)
    else:
        acc_ref[...] = carry[0][...]
        m_ref[...] = carry[1][...]
        l_ref[...] = carry[2][...]

    total = jnp.int32(0)
    for i, (kind, _) in enumerate(chunks):
        row = row_of(kind)
        for b in range(per):
            first = sc[order + sc[4] * per + b] * blk

            state = list(cached[i])
            least = jnp.minimum(first, sc[2 + row] - 1)
            most = jnp.minimum(first + blk, sc[2 + row]) - 1
            for base in fresh_runs[i]:
                state[0] = state[0] | (base <= most).astype(jnp.int32)
                state[1] = state[1] | (base + blk - 1 > least).astype(jnp.int32)
            go = jnp.where(first < sc[2 + row], state[0], 0)
            for h in range(heads):
                work[0, total] = (h * rows + row) * per + b
                work[1, total] = h * len(chunks) + i
                work[2, total] = state[1]
                work[3, total] = first
                work[4, total] = i
                total = total + go
    none = len(chunks)
    for run in range(runs):
        for j, value in enumerate((0, 0, -1)):
            work[run_at + 3 * run + j, none] = value
    work[0, total] = work[0, jnp.maximum(total - 1, 0)]
    for extra in range(1, 4):
        work[0, total + extra] = 0
    for extra in range(4):
        work[1, total + extra] = 0
        work[2, total + extra] = 1
        work[3, total + extra] = 0
        work[4, total + extra] = none

    lanes = min(lane_step, width)

    def prepare(at, s_ref, t_ref, start):
        tile = work[0, at]
        h, r, b = tile // tiles, (tile // per) % rows, tile % per
        heads_at = pl.ds(pl.multiple_of((first_head + h) * group, group), group)
        tokens_at = pl.ds(b * blk + start // group, lanes // group)
        q = q_ref[r, tokens_at, heads_at, :].reshape(lanes, size)
        scores(q, kbuf[work[1, at]], s_ref, t_ref, slice(start, start + lanes))

    def fix(at, s_ref, t_ref):
        @pl.when(work[2, at] == 1)
        def _():
            i = work[4, at]
            token = work[3, at] + lax.broadcasted_iota(jnp.int32, (1, width), 1) // group
            run = lambda k: [work[run_at + 3 * k + j, i] for j in range(3)]
            hide(token, run, runs, s_ref, t_ref)

    def finish(at, s_ref, t_ref, start):
        spot = slice(start, start + lanes)
        absorb(work[0, at], vt_ref[work[1, at]], s_ref, t_ref, m_ref, l_ref, acc_ref, spot)

    starts = range(0, width, lanes)

    @pl.when(total > 0)
    def _():
        for start in starts:
            prepare(0, s0, t0, start)
        for start in starts:
            prepare(1, s1, t1, start)
        fix(0, s0, t0)
        fix(1, s1, t1)

    def advance(at, now, later):
        for k in range(2):
            for start in starts:
                prepare(at + 2 + k, *later[k], start)
                finish(at + k, *now[k], start)
        for k in range(2):
            fix(at + 2 + k, *later[k])

    even, odd = ((s0, t0), (s1, t1)), ((s2, t2), (s3, t3))

    def body(i, _):
        @pl.when(i % 2 == 0)
        def _():
            advance(2 * i, even, odd)

        @pl.when(i % 2 == 1)
        def _():
            advance(2 * i, odd, even)

        return 0

    lax.fori_loop(0, (total + 1) // 2, body, 0)

    if last:

        def write(tile):
            h, r, b = tile // tiles, (tile // per) % rows, tile % per
            heads_at = pl.ds(pl.multiple_of((first_head + h) * group, group), group)
            return pltpu.make_async_copy(
                stage.at[tile], o_ref.at[r, pl.ds(b * blk, blk), heads_at], o_sem.at[tile]
            )

        def store(tile, _):
            r, b = (tile // per) % rows, tile % per
            first = sc[order + sc[4] * per + b] * blk
            live = sc[2 + r]

            @pl.when(first >= live)
            def _():
                stage[tile] = jnp.zeros(stage.shape[1:], stage.dtype)

            @pl.when(first < live)
            def _():
                sums = over_sublanes(jnp.add, l_ref[tile])
                out = (acc_ref[tile].reshape(-1, 8, width) / sums).reshape(size, width)
                query = lax.broadcasted_iota(jnp.int32, (1, width), 1)
                out = jnp.where(query < (live - first) * group, out, 0.0)
                stage[tile] = out.astype(stage.dtype).T.reshape(stage.shape[1:])

            write(tile).start()
            return 0

        lax.fori_loop(0, heads * tiles, store, 0)
        lax.fori_loop(0, heads * tiles, lambda t, _: (write(t).wait(), 0)[1], 0)


def step_call(scalars, q_rot, carry, parts, chunks, out, last, first_head, blocks, n, group):
    rows, count, _, size = q_rot.shape
    sources = sorted({source for _, units in chunks for source, _ in units})
    packed = tuple(not isinstance(parts[source], tuple) for source in sources)
    arrays = []
    for source in sources:
        arrays += list(parts[source]) if isinstance(parts[source], tuple) else [parts[source]]
    unit_heads = arrays[0].shape[-3]
    per = blocks // n
    blk = count // per
    width = blk * group
    tiles = unit_heads * rows * per
    depth = chunk_units * count
    items = unit_heads * per * len(chunks)
    fresh, chained = carry is None, last and out is not None
    vmem, anywhere = pl.BlockSpec(memory_space=pltpu.VMEM), pl.BlockSpec(memory_space=pl.ANY)
    state = lambda d: (tiles, d, width)
    f32 = lambda d: jax.ShapeDtypeStruct(state(d), jnp.float32)
    scratch = [
        pltpu.VMEM((unit_heads * len(chunks), depth, size), jnp.bfloat16),
        pltpu.VMEM((unit_heads * len(chunks), size, depth), jnp.bfloat16),
        *[pltpu.VMEM((depth, width), jnp.float32) for _ in range(4)],
        *[pltpu.VMEM((8, width), jnp.float32) for _ in range(4)],
        pltpu.SMEM((5 + 3 * depth // blk, items + 4), jnp.int32),
    ]
    operands = [scalars, q_rot] + ([] if fresh else list(carry)) + arrays
    specs = [pl.BlockSpec(memory_space=pltpu.SMEM)] + [vmem] * (len(operands) - 1)
    aliases = {} if fresh or last else {2: 0, 3: 1, 4: 2}
    if last:
        scratch += [
            pltpu.VMEM((tiles, blk, group, size), jnp.bfloat16),
            pltpu.SemaphoreType.DMA((tiles,)),
        ] + [pltpu.VMEM(state(d), jnp.float32) for d in (size, 8, 8)]
        if chained:
            operands.append(out)
            specs.append(anywhere)
            aliases = {len(operands) - 1: 0}
        shapes, out_specs = jax.ShapeDtypeStruct(q_rot.shape, q_rot.dtype), anywhere
    else:
        shapes, out_specs = [f32(size), f32(8), f32(8)], [vmem] * 3
    cfg = (n, blocks, blk, first_head, chunks, sources, packed, fresh, last, chained)
    pairs = items * depth * width
    return pl.pallas_call(
        functools.partial(step_kernel, cfg),
        in_specs=specs,
        out_specs=out_specs,
        scratch_shapes=scratch,
        out_shape=shapes,
        input_output_aliases=aliases,
        compiler_params=pltpu.CompilerParams(vmem_limit_bytes=24 * 1024 * 1024),
        cost_estimate=pl.CostEstimate(
            flops=pairs * size * 4, bytes_accessed=1024 * 1024, transcendentals=pairs
        ),
    )(*operands)


def turn_kernel(parts, q_ref, cosine_ref, sine_ref, o_ref):
    i = pl.program_id(0)
    tokens, _, size = q_ref.shape[1:]
    x = q_ref[0].astype(jnp.float32)
    cosine = cosine_ref[0][:, None, :]
    sine = sine_ref[0][:, None, :]
    turned = x * cosine + pltpu.roll(x, size // 2, 2) * sine
    at = pl.ds(pl.multiple_of((i % parts) * tokens, tokens), tokens)
    o_ref[i // parts, at] = turned.astype(o_ref.dtype)


def turn_call(queries, cosine, sine):
    rows, count, heads, size = queries.shape
    tokens = count // 4
    parts = count // tokens
    table = pl.BlockSpec((1, tokens, size), lambda i: (i // parts, i % parts, 0))
    return pl.pallas_call(
        functools.partial(turn_kernel, parts),
        grid=(rows * parts,),
        in_specs=[
            pl.BlockSpec((1, tokens, heads, size), lambda i: (i // parts, i % parts, 0, 0)),
            table,
            table,
        ],
        out_specs=pl.BlockSpec(queries.shape, lambda i: (0, 0, 0, 0)),
        out_shape=jax.ShapeDtypeStruct(queries.shape, queries.dtype),
        compiler_params=pltpu.CompilerParams(vmem_limit_bytes=10 * 1024 * 1024),
        cost_estimate=pl.CostEstimate(
            flops=queries.size * 4, bytes_accessed=queries.size * 4, transcendentals=0
        ),
        name="turn",
    )(pltpu.with_memory_space_constraint(queries, pltpu.HBM), cosine, sine)


def shards(
    ring,
    queries,
    span_key_rows,
    span_value_rows,
    prefix_key_rows,
    prefix_value_rows,
    cached_len,
    new_len,
    prefill_flag,
    block_order,
):
    n = len(ring)
    rows, count, heads, size = queries.shape
    kv_heads = span_key_rows.shape[2]
    group = heads // kv_heads
    blocks = block_order.shape[0]
    per = blocks // n
    blk = count // per
    ctx = lax.axis_index("ctx")

    partial = jnp.where(prefill_flag[0] == 0, 0, 1).astype(jnp.int32)
    half = size // 2
    mine = lax.dynamic_slice(block_order, (ctx * per,), (per,))
    q_index = (mine[:, None] * blk + jnp.arange(blk, dtype=jnp.int32)[None, :]).reshape(count)
    base = jnp.where(prefill_flag == 1, 0, cached_len)
    positions = base[:, None] + q_index[None, :]
    inverse = rope_base ** (-(jnp.arange(half, dtype=jnp.float32) * 2.0 / size))
    angle = positions.astype(jnp.float32)[:, :, None, None] * inverse
    cosine = jnp.cos(angle)
    sine = jnp.sin(angle)
    unit = -(-kv_heads // streams)

    def payload(at):
        pick = lambda x: jnp.swapaxes(jnp.where(partial == 0, x[0], x[1])[:, at], 0, 1)
        new = lambda x: jnp.moveaxis(x, 2, 0).reshape(x.shape[2], rows * count, size)
        keys = new(rotate(span_key_rows[:, :, at], cosine, sine))
        values = new(span_value_rows[:, :, at])
        return jnp.stack(
            [
                jnp.concatenate([pick(prefix_key_rows), keys], 1),
                jnp.concatenate([pick(prefix_value_rows), values], 1),
            ]
        )

    both = lambda x, y: jnp.concatenate([x[:, :, 0], y[:, :, 0]], -1)
    q_rot = turn_call(queries, both(cosine, cosine), both(-sine, sine))

    place = {c: i for i, c in enumerate(ring)}
    table = jnp.array(
        [[ring[(place[c] - s) % n] for s in range(n)] for c in range(n)], jnp.int32
    )
    sources = lax.dynamic_slice(table, (ctx, 0), (1, n)).reshape(n)
    live = jnp.where(partial == 0, cached_len[0], cached_len[1])
    scalars = jnp.concatenate([partial[None], live[None], new_len, sources, block_order])

    forward = [(ring[i], ring[(i + 1) % n]) for i in range(n)]
    backward = [(b, a) for a, b in forward]

    def send(x, way):
        return lax.ppermute(x, "ctx", way)

    firsts = list(range(0, kv_heads, unit))
    count_u = len(firsts)
    own = [payload(slice(h, h + unit)) for h in firsts]
    ahead, back, carry = list(own), list(own), [None] * count_u
    out = None

    parts = [{0: own[u]} for u in range(count_u)]
    local = prefix_key_rows.shape[1]
    steps = plan(n, local // count)

    def step(u, s, last=False):
        return step_call(
            scalars,
            q_rot,
            carry[u],
            parts[u],
            steps[s],
            out,
            last,
            firsts[u],
            blocks,
            n,
            group,
        )

    for u in range(count_u):
        ahead[u], back[u] = send(ahead[u], forward), send(back[u], backward)
    for u in range(count_u):
        carry[u] = step(u, 0)
    for s in range(1, n // 2):
        for u in range(count_u):
            here, there = ahead[u], back[u]
            parts[u][s], parts[u][n - s] = here, there
            if s + 1 == n // 2:
                here, there = here[0], there[1]
            ahead[u], back[u] = send(here, forward), send(there, backward)
            carry[u] = step(u, s)
    for u in range(count_u):
        parts[u][n // 2] = (ahead[u], back[u])
        out = step(u, n // 2, last=True)
    return out


def solution(mesh):
    ring = ring_order(mesh)
    return jax.shard_map(
        functools.partial(shards, ring),
        mesh=mesh,
        in_specs=(
            P("batch", "ctx", "tp", None),
            P("batch", "ctx", "tp", None),
            P("batch", "ctx", "tp", None),
            P("batch", "ctx", "tp", None),
            P("batch", "ctx", "tp", None),
            P("batch"),
            P("batch"),
            P("batch"),
            P(),
        ),
        out_specs=P("batch", "ctx", "tp", None),
        check_vma=False,
    )
```
